32 devices in a mesh: lon: 8 (over z, x), lat: 4 (over y, core).
Axes of the slice: x: 2, y: 2, z: 4, core: 2. Of those that a mesh axis runs over, the one named last changes fastest.
Arguments:
- control_fields: float32 [2, 4, 544, 1536], P(None, None, 'lon', 'lat'), may hold values from -4 to 4
- unexplained_elevation: float32 [544, 1536], P('lon', 'lat'), may hold values from -6 to 6
- diffusivity: float32 [544, 1536], P('lon', 'lat'), may hold values from 0.15 to 0.49
- depth_levels: int32 [544, 1536], P('lon', 'lat'), may hold values from 0 to 4
- fold_partner: int32 [544], replicated, may hold values from 0 to 543, as said below
- prior_sigmas: float32 [2, 4], replicated, may hold values from 0.5 to 2
- haline_thermal_ratio: float32 [544, 1536], P('lon', 'lat'), may hold values from -0.6 to 0.6
- expansion_coefficients: float32 [2, 4], replicated, may hold values from -3 to 3
Outputs:
- state_fields: float32 [2, 4, 544, 1536], P(None, None, 'lon', 'lat')
- sea_height: float32 [544, 1536], P('lon', 'lat')
The draws below stay inside these ranges and needn't reach their ends.
Inputs may be any that keep to these rules, and one draw needn't show every extreme that they name: `fold_partner`: column i's fold partner lies in the block of 68 columns with block index (8 - (i div 68)) mod (8); within one block the partners are distinct.
All inputs are finite; a program needn't handle non-finite values.
Results may differ from the reference program's by a relative error of at most 0.0003.
Values sent between devices are 32-bit elements; how exact they have to be, the bound alone decides.
A program may use at most 64 MiB of HBM per device.

```python
import math
import jax
import jax.numpy as jnp
from jax import lax

DEPTH_STRATA = 4
CLON = 68
PASSES = 4
NLON = 544
NLAT = 1536


def draw_control_fields(key, part):
    rough_part = jax.random.normal(key, (2, DEPTH_STRATA, NLON, NLAT), jnp.float32)
    return jnp.clip(rough_part, -4.0, 4.0)


def draw_fold_partner(key, part):
    blocks = NLON // CLON
    block_keys = jax.random.split(key, blocks)
    orders = jax.vmap(lambda one_key: jax.random.permutation(one_key, CLON))(block_keys)
    mirror = ((blocks - jnp.arange(blocks, dtype=jnp.int32)) % blocks)[:, None] * CLON
    return (mirror + orders.astype(jnp.int32)).reshape(NLON)


def place_ends(values, rng, low, top_value):
    spot = [jax.random.randint(jax.random.fold_in(rng, axis), (), 0, length) for axis, length in enumerate(values.shape)]
    main_axis = values.shape.index(max(values.shape))
    neighbour = spot[:main_axis] + [(spot[main_axis] + 1) % values.shape[main_axis]] + spot[main_axis + 1:]
    return values.at[tuple(spot)].set(low).at[tuple(neighbour)].set(top_value)


def levels(rng, extent, cuts, smallest, largest):
    loudness = 1.0
    for axis_at, blocks in cuts:
        heights = jax.random.uniform(jax.random.fold_in(jax.random.fold_in(rng, 6), axis_at), (blocks,), jnp.float32, smallest / len(cuts), largest / len(cuts))
        loudness = loudness * jnp.repeat(jnp.exp(heights), extent[axis_at] // blocks).reshape((-1,) + (1,) * (len(extent) - 1 - axis_at))
    return loudness


def centred(key, dims, deviation, limit, shards=(), kind=jnp.bfloat16):
    result = jax.random.normal(key, dims, jnp.float32) * deviation
    if len(shards) > 0:
        result = levels(key, dims, shards, -0.22, 0.18) * result
    return jnp.clip(result, min=-limit, max=limit).astype(kind)


def setup_inputs(seed: int = 0) -> dict:
    streams_of = jax.random.split(jax.random.key(seed), 9)
    control_fields = draw_control_fields(jax.random.fold_in(streams_of[8], 71), 0)
    unexplained_elevation = centred(streams_of[1], (NLON, NLAT), 1.0, 6.0, ((0, 8), (1, 4)), jnp.float32)
    diffusivity = jnp.clip(jnp.exp(math.log(0.49) - 1.1837701 * jax.random.uniform(streams_of[2], (NLON, NLAT), jnp.float32) ** levels(streams_of[2], (NLON, NLAT), ((0, 8), (1, 4)), -0.2, 0.2)), 0.15, 0.49)
    depth_levels = place_ends(jax.random.randint(streams_of[3], (NLON, NLAT), 0, DEPTH_STRATA + 1), jax.random.fold_in(streams_of[3], 1), 0, DEPTH_STRATA).astype(jnp.int32)
    fold_partner = draw_fold_partner(jax.random.fold_in(streams_of[8], 71), 0)
    prior_sigmas = jnp.clip(jnp.exp(jax.random.uniform(streams_of[5], (2, DEPTH_STRATA), jnp.float32, math.log(0.5), math.log(2.0))), 0.5, 2.0)
    haline_thermal_ratio = jnp.clip(jax.random.uniform(streams_of[6], (NLON, NLAT), jnp.float32, -0.6, 0.6) * levels(streams_of[6], (NLON, NLAT), ((0, 8), (1, 4)), -0.4, 0.0), -0.6, 0.6)
    expansion_coefficients = centred(streams_of[7], (2, DEPTH_STRATA), 0.3, 3.0, (), jnp.float32)
    return {"control_fields": control_fields, "unexplained_elevation": unexplained_elevation, "diffusivity": diffusivity, "depth_levels": depth_levels, "fold_partner": fold_partner, "prior_sigmas": prior_sigmas, "haline_thermal_ratio": haline_thermal_ratio, "expansion_coefficients": expansion_coefficients}


def reference(control_fields, unexplained_elevation, diffusivity, depth_levels, fold_partner, prior_sigmas, haline_thermal_ratio, expansion_coefficients):
    kappa_east = jnp.roll(diffusivity, -1, axis=0)
    kappa_north = jnp.concatenate([diffusivity[:, 1:], diffusivity[fold_partner, -1:]], axis=1)

    def lone_stratum(ocean_elevation, level_index):
        wet_cells = (level_index < depth_levels).astype(jnp.float32)
        wet_east = jnp.roll(wet_cells, -1, axis=0)
        wet_north = jnp.concatenate([wet_cells[:, 1:], wet_cells[fold_partner, -1:]], axis=1)
        east_face = diffusivity * kappa_east * wet_cells * wet_east
        west_face = jnp.roll(east_face, 1, axis=0)
        north_face = diffusivity * kappa_north * wet_cells * wet_north
        south_face = jnp.concatenate([jnp.zeros_like(north_face[:, :1]), north_face[:, :-1]], axis=1)
        stratum_entries = lax.dynamic_index_in_dim(control_fields, level_index, 1, keepdims=False) * wet_cells
        for repeat in range(PASSES):
            east_value = jnp.roll(stratum_entries, -1, axis=1)
            west_value = jnp.roll(stratum_entries, 1, axis=1)
            north_value = jnp.concatenate([stratum_entries[:, :, 1:], stratum_entries[:, fold_partner, -1:]], axis=2)
            south_value = jnp.concatenate([jnp.zeros_like(stratum_entries[:, :, :1]), stratum_entries[:, :, :-1]], axis=2)
            stratum_entries = (stratum_entries + east_face * (east_value - stratum_entries)
                           + west_face * (west_value - stratum_entries)
                           + north_face * (north_value - stratum_entries)
                           + south_face * (south_value - stratum_entries))
        sigma_factor = lax.dynamic_index_in_dim(prior_sigmas, level_index, 1, keepdims=False)
        expansion_pair = lax.dynamic_index_in_dim(expansion_coefficients, level_index, 1, keepdims=False)
        thermal_grid = sigma_factor[0] * stratum_entries[0]
        saltiness_grid = sigma_factor[1] * stratum_entries[1] + haline_thermal_ratio * thermal_grid
        ocean_elevation = ocean_elevation + (expansion_pair[0] * thermal_grid + expansion_pair[1] * saltiness_grid)
        return ocean_elevation, (thermal_grid, saltiness_grid)

    ocean_elevation, (thermal_columns, saltiness_columns) = lax.scan(lone_stratum, unexplained_elevation, jnp.arange(DEPTH_STRATA, dtype=jnp.int32))
    return jnp.stack([thermal_columns, saltiness_columns]), ocean_elevation
```

```python
import functools

import jax
import jax.numpy as jnp
from jax import lax
from jax.experimental import pallas as pl
from jax.experimental.pallas import tpu as pltpu
from jax.sharding import PartitionSpec as P

PASSES = 4
LANES = 128
GROUP = LANES // PASSES
STRAIGHT_ROWS = (1, 2, 3, 2, 1)
MIRROR_ROWS = (2, 3, 4, 3, 2)
MESH = pl.DeviceIdType.MESH
F32 = jnp.float32


def strip_pieces(rows):
    return rows + (rows + 1) // 2


def iotas():
    shape = (8, LANES)
    return lax.broadcasted_iota(jnp.int32, shape, 1), lax.broadcasted_iota(jnp.int32, shape, 0)


def take(values, index):
    return jnp.take_along_axis(values, index, axis=1, mode="promise_in_bounds")


def roll(values, shift):
    shift = shift % LANES
    return pltpu.roll(values, shift, 1) if shift else values


def make_strip(p_src, q_src):
    lane, sub = iotas()
    p = [p_src[0, m] for m in range(5)]
    weights_tail = roll(p[4], -4 * PASSES)

    def row(r, parts):
        index = PASSES * (lane % GROUP) + (PASSES - 1 - r)
        picked = [take(part, index) for part in parts]
        return jnp.where(lane < GROUP, picked[0], jnp.where(lane < 2 * GROUP, picked[1], picked[2]))

    for t in range(2):
        first, second = (row(2 * t + h, (p[2], p[3], weights_tail)) for h in range(2))
        q_src[3 * t] = jnp.where(sub < 4, first, second)
        for h in range(2):
            q_src[3 * t + 1 + h] = row(2 * t + h, (p[0], p[1], p[4]))


def fold_strip(n_lon, lon_cells, b, q_src, q_land, fp_s, p_land, c_land):
    lane, sub = iotas()

    kinds = {"S": STRAIGHT_ROWS, "M": MIRROR_ROWS}
    blocks = {
        (kind, o): lax.rem((b if kind == "S" else -b) + o + 2 * n_lon, n_lon) for kind in kinds for o in range(-2, 3)
    }

    def collect(l, rows):
        return tuple(
            jnp.where(lane == l, fp_s[block * lon_cells + l] - lax.rem(n_lon - block, n_lon) * lon_cells, row)
            for block, row in zip(blocks.values(), rows)
        )

    nothing = jnp.zeros((8, LANES), jnp.int32)
    index = dict(zip(blocks, lax.fori_loop(0, lon_cells, collect, (nothing,) * len(blocks))))
    y, kw = {}, {}
    for kind, rows in kinds.items():
        for o in range(-2, 3):
            slot = o + 2 + (0 if kind == "S" else 5)
            piece = (lambda i: q_src[i]) if slot == 2 else (lambda i, slot=slot: q_land[slot, i])
            for r in range(rows[o + 2]):
                t, h = r // 2, r % 2
                pair = piece(3 * t)
                turned = pltpu.roll(pair, 4, 0)
                kw[kind, o, r] = jnp.where((sub < 4) if h == 0 else (sub >= 4), pair, turned)
                y[kind, o, r] = piece(3 * t + 1 + h)

    other = {"S": "M", "M": "S"}

    def sides(table, kind, o, r):
        here = table[kind, o, r]
        from_east = table.get((kind, o + 1, r), here)
        from_west = table.get((kind, o - 1, r), here)
        return jnp.where(lane == lon_cells - 1, roll(from_east, lon_cells - 1), roll(here, -1)) + jnp.where(
            lane == 0, roll(from_west, 1 - lon_cells), roll(here, 1)
        )

    def above(table, kind, o, r):
        if r:
            return table[kind, o, r - 1]
        return take(table[other[kind], -o, 0], index[kind, o])

    def around(table, kind, o, r):
        return sides(table, kind, o, r) + above(table, kind, o, r) + table[kind, o, r + 1]

    def ghost_row(table):
        own = take(table["M", 0, 0], index["S", 0])
        right = take(table["M", -1, 0], index["S", 1])
        left = take(table["M", 1, 0], index["S", -1])
        result = jnp.where(
            lane < 4, roll(left, 4 - lon_cells), jnp.where(lane < 4 + lon_cells, roll(own, 4), roll(right, 4 + lon_cells))
        )
        return jnp.where(lane < 8 + lon_cells, result, 0.0)

    ghost_kw = ghost_row(kw)
    ghosts = [ghost_row(y)]
    coefficients = {}
    for step in range(1, PASSES):
        renewed = {}
        for kind, rows in kinds.items():
            for o in range(-2, 3):
                for r in range(rows[o + 2] - step):
                    if (kind, o, r) not in coefficients:
                        k0 = kw[kind, o, r]
                        coefficients[kind, o, r] = 1.0 - k0 * around(kw, kind, o, r), k0 * k0
                    c, q = coefficients[kind, o, r]
                    renewed[kind, o, r] = c * y[kind, o, r] + q * around(y, kind, o, r)
        y.update(renewed)
        ghosts.append(ghost_row(y))

    def packed(column):
        index = column + 4 + lane // PASSES
        result = take(ghosts[0], index)
        for s in range(1, PASSES):
            result = jnp.where(lane % PASSES == s, take(ghosts[s], index), result)
        return result

    def packed_kw(column):
        return jnp.where(lane % PASSES == 0, take(ghost_kw, column + 4 + lane // PASSES), 0.0)

    def edge(column):
        return jnp.where(lane < 4 * PASSES, packed(column), roll(packed_kw(column), 4 * PASSES))

    for m in range(2):
        p_land[1, m] = packed(GROUP * m)
        p_land[1, 2 + m] = packed_kw(GROUP * m)
    p_land[1, 4] = edge(2 * GROUP)
    c_land[2] = edge(-4)
    c_land[3] = edge(lon_cells)


def diffuse_kernel(
    n_lon, n_lat,
    x_hbm, k_hbm, d_hbm, fp_hbm,
    y_out,
    x_v, k_v, d_v, fp_s,
    y0, y1, y2, y3, kw, cc, qq,
    kd_src, x_land, kd_land, p_src, p_land, c_land, q_src, q_land,
    local_sem, send_sem, recv_sem,
):
    lon_cells, lat_cells = k_hbm.shape
    rows = lon_cells + 2 * PASSES
    tiles = lat_cells // LANES
    edge = lat_cells
    b = lax.axis_index("lon")
    a = lax.axis_index("lat")
    has_n = a < n_lat - 1
    has_s = a > 0
    is_top = a == n_lat - 1
    east = lax.rem(b + 1, n_lon)
    west = lax.rem(b + n_lon - 1, n_lon)
    north = lax.rem(a + 1, n_lat)
    south = lax.rem(a + n_lat - 1, n_lat)
    lane, sub = iotas()
    level = sub % 4

    straight = [
        (slot, STRAIGHT_ROWS[slot], lax.rem(b - (slot - 2) + n_lon, n_lon)) for slot in (0, 1, 3, 4)
    ]
    mirrored = [
        (5 + slot, MIRROR_ROWS[slot], lax.rem((slot - 2) - b + 2 * n_lon, n_lon)) for slot in range(5)
    ]

    barrier = pltpu.get_barrier_semaphore()

    def hail(lon, lat):
        pl.semaphore_signal(barrier, inc=1, device_id={"lon": lon, "lat": lat}, device_id_type=MESH)

    hail(west, a)
    hail(east, a)

    @pl.when(has_n)
    def _():
        for lon in (b, east, west):
            hail(lon, north)

    @pl.when(has_s)
    def _():
        for lon in (b, east, west):
            hail(lon, south)

    @pl.when(is_top)
    def _():
        for _, _, target in straight:
            hail(target, a)
        for _, _, target in mirrored:
            @pl.when(target != b)
            def _():
                hail(target, a)

    expected = 2 + jnp.where(has_n, 3, 0) + jnp.where(has_s, 3, 0) + jnp.where(is_top, 4, 0)
    for _, _, target in mirrored:
        expected = expected + jnp.where(jnp.logical_and(is_top, target != b), 1, 0)

    chunks = x_v.shape[1] // 17
    load_k = pltpu.make_async_copy(k_hbm, k_v, local_sem.at[0])
    load_d = pltpu.make_async_copy(d_hbm, d_v, local_sem.at[1])
    load_fp = pltpu.make_async_copy(fp_hbm, fp_s, local_sem.at[2])
    loads = [
        pltpu.make_async_copy(
            x_hbm.at[:, pl.ds(17 * n, 17)], x_v.at[:, pl.ds(17 * n, 17)], local_sem.at[3 + n]
        )
        for n in range(chunks)
    ]
    for copy in [load_k, load_d, *loads, load_fp]:
        copy.start()

    def remote(src, dst, index, lon, lat):
        return pltpu.make_async_remote_copy(
            src_ref=src, dst_ref=dst, send_sem=send_sem.at[index], recv_sem=recv_sem.at[index],
            device_id={"lon": lon, "lat": lat}, device_id_type=MESH,
        )

    along = [
        remote(x_hbm.at[:, pl.ds(lon_cells - 4, 4)], x_land.at[0], 0, east, a),
        remote(x_hbm.at[:, pl.ds(0, 4)], x_land.at[1], 1, west, a),
        remote(kd_src.at[0], kd_land.at[0], 2, east, a),
        remote(kd_src.at[1], kd_land.at[1], 3, west, a),
    ]
    up = [
        remote(p_src.at[0, pl.ds(0, 5)], p_land.at[0, pl.ds(0, 5)], 4, b, north),
        remote(p_src.at[0, 4], c_land.at[0], 6, east, north),
        remote(p_src.at[0, 5], c_land.at[1], 7, west, north),
    ]
    down = [
        remote(p_src.at[1, pl.ds(0, 5)], p_land.at[1, pl.ds(0, 5)], 5, b, south),
        remote(p_src.at[1, 4], c_land.at[2], 8, east, south),
        remote(p_src.at[1, 5], c_land.at[3], 9, west, south),
    ]

    def strip(slot, count, target):
        part = pl.ds(0, strip_pieces(count))
        return remote(q_src.at[part], q_land.at[slot, part], 10 + slot, target, a)

    strip_straight = [strip(*which) for which in straight]
    strip_mirrored = [(which[2] != b, strip(*which), which[0]) for which in mirrored]

    load_k.wait()
    load_d.wait()
    kd_src[0, 0:4] = k_v[lon_cells - 4 : lon_cells, :]
    kd_src[0, 4:8] = d_v[lon_cells - 4 : lon_cells, :].astype(F32)
    kd_src[1, 0:4] = k_v[0:4, :]
    kd_src[1, 4:8] = d_v[0:4, :].astype(F32)

    pl.semaphore_wait(barrier, expected)
    for copy in along:
        copy.start()

    wide_level = lax.broadcasted_iota(jnp.int32, (8, lat_cells), 0) % 4

    def own_weights(i, carry):
        k = jnp.broadcast_to(k_v[pl.ds(i, 1), :], (8, lat_cells))
        d = jnp.broadcast_to(d_v[pl.ds(i, 1), :], (8, lat_cells))
        kw[i + PASSES, :, 0:edge] = jnp.where(d > wide_level, k, 0.0)
        return carry

    lax.fori_loop(0, lon_cells, own_weights, 0, unroll=17)
    for copy in loads:
        copy.wait()

    def own_fields(i, carry):
        x = jnp.concatenate([x_v[0, i], x_v[1, i]], axis=0)
        y0[i + PASSES, :, 0:edge] = x * kw[i + PASSES, :, 0:edge]
        return carry

    lax.fori_loop(0, lon_cells, own_fields, 0, unroll=17)

    for side in range(2):
        columns = slice(edge - LANES, edge) if side == 0 else slice(0, LANES)
        first = PASSES if side == 0 else 0

        def pack(ref, start, count, offset=0):
            result = jnp.zeros((8, LANES), F32)
            for g in range(count):
                at = PASSES * g + offset
                moved = roll(ref[PASSES + start + g, :, columns], first + at)
                result = jnp.where(jnp.logical_and(lane >= at, lane < at + PASSES), moved, result)
            return result

        heads = {}
        for m in range(2):
            for place, ref in ((m, y0), (2 + m, kw)):
                heads[place] = pack(ref, GROUP * m, GROUP)
                p_src[side, place] = heads[place]
        p_src[side, 4] = pack(y0, 2 * GROUP, 4) + pack(kw, 2 * GROUP, 4, 4 * PASSES)
        p_src[side, 5] = jnp.where(lane < 4 * PASSES, heads[0], roll(heads[2], 4 * PASSES))

    @pl.when(has_n)
    def _():
        for copy in up:
            copy.start()

    @pl.when(has_s)
    def _():
        for copy in down:
            copy.start()

    load_fp.wait()

    @pl.when(is_top)
    def _():
        make_strip(p_src, q_src)
        for copy in strip_straight:
            copy.start()
        for away, copy, slot in strip_mirrored:
            @pl.when(away)
            def _():
                copy.start()

            @pl.when(jnp.logical_not(away))
            def _():
                q_land[slot] = q_src[...]

    @pl.when(has_s)
    def _():
        up[0].wait_recv()

    @pl.when(jnp.logical_not(has_s))
    def _():
        p_land[0] = jnp.zeros(p_land.shape[1:], F32)
        for n in range(2):
            c_land[n] = jnp.zeros((8, LANES), F32)

    @pl.when(has_n)
    def _():
        down[0].wait_recv()

    @pl.when(is_top)
    def _():
        for copy in strip_straight:
            copy.wait_recv()
        for away, copy, _ in strip_mirrored:
            @pl.when(away)
            def _():
                copy.wait_recv()
        fold_strip(n_lon, lon_cells, b, q_src, q_land, fp_s, p_land, c_land)

    def spread(ref, row, southern, northern, at):
        ref[row, :, edge : edge + LANES] = jnp.where(
            lane < PASSES, roll(northern, -at), jnp.where(lane >= LANES - PASSES, roll(southern, -PASSES - at), 0.0)
        )

    for m in range(2):
        for place, ref in ((m, y0), (2 + m, kw)):
            southern, northern = p_land[0, place], p_land[1, place]
            for g in range(GROUP):
                spread(ref, PASSES + GROUP * m + g, southern, northern, PASSES * g)

    def spread_four(row, southern, northern):
        for g in range(4):
            spread(y0, row + g, southern, northern, PASSES * g)
            spread(kw, row + g, southern, northern, PASSES * (g + 4))

    spread_four(PASSES + 2 * GROUP, p_land[0, 4], p_land[1, 4])

    held = jnp.where(is_top, PASSES, 0)

    def lattice(ref, row, turn=None):
        here = [ref[row, :, LANES * t : LANES * (t + 1)] for t in range(tiles + 1)]
        up_one = [roll(v, -1) for v in here]
        down_one = [roll(v, 1) for v in here]
        over = up_one[tiles] if turn is None else pltpu.roll(here[tiles], turn, 1)
        sums = []
        for t in range(tiles + 1):
            after = over if t == tiles - 1 else up_one[(t + 1) % (tiles + 1)]
            n = jnp.where(lane == LANES - 1, after, up_one[t])
            s = jnp.where(lane == 0, down_one[t - 1], down_one[t])
            at = slice(LANES * t, LANES * (t + 1))
            sums.append((n + s) + (ref[row + 1, :, at] + ref[row - 1, :, at]))
        return here, sums

    def coefficients(row):
        here, sums = lattice(kw, row)
        for t in range(tiles + 1):
            c = 1.0 - here[t] * sums[t]
            q = here[t] * here[t]
            if t == tiles:
                c = jnp.where(lane < held, 1.0, c)
                q = jnp.where(lane < held, 0.0, q)
            cc[row, :, LANES * t : LANES * (t + 1)] = c
            qq[row, :, LANES * t : LANES * (t + 1)] = q

    states = [y0, y1, y2, y3]

    def advance(step, row):
        turn = jnp.where(is_top, LANES - 1 - step, LANES - 1)
        here, sums = lattice(states[step], row, turn)
        for t in range(tiles + (step < PASSES - 1)):
            at = slice(LANES * t, LANES * (t + 1))
            new = cc[row, :, at] * here[t] + qq[row, :, at] * sums[t]
            if step < PASSES - 1:
                states[step + 1][row, :, at] = new
            else:
                y_out[row - PASSES, :, at] = new

    def over_rows(first, last, body, unroll):
        def one(row, carry):
            body(row)
            return carry

        lax.fori_loop(first, last, one, 0, unroll=unroll)

    over_rows(PASSES + 1, rows - PASSES - 1, coefficients, 33)
    for step in range(PASSES):
        over_rows(PASSES + 1 + step, rows - PASSES - 1 - step, functools.partial(advance, step), 33 - step)

    for copy in along:
        copy.wait_recv()

    @pl.when(has_s)
    def _():
        for copy in up[1:]:
            copy.wait_recv()

    @pl.when(has_n)
    def _():
        for copy in down[1:]:
            copy.wait_recv()

    for side, row in ((0, 0), (1, rows - PASSES)):
        for g in range(4):
            k = jnp.broadcast_to(kd_land[side, g : g + 1, :], (8, lat_cells))
            d = jnp.broadcast_to(kd_land[side, 4 + g : 5 + g, :], (8, lat_cells))
            w = jnp.where(d > wide_level.astype(F32), k, 0.0)
            kw[row + g, :, 0:edge] = w
            x = jnp.concatenate([x_land[side, 0, g], x_land[side, 1, g]], axis=0)
            y0[row + g, :, 0:edge] = x * w
        spread_four(row, c_land[side], c_land[2 + side])

    def both_ends(first, body):
        def one(n, carry):
            body(first + n)
            body(rows - 1 - first - n)
            return carry

        lax.fori_loop(0, PASSES, one, 0, unroll=PASSES)

    both_ends(1, coefficients)
    for step in range(PASSES):
        both_ends(1 + step, functools.partial(advance, step))

    for copy in along:
        copy.wait_send()

    @pl.when(has_n)
    def _():
        for copy in up:
            copy.wait_send()

    @pl.when(has_s)
    def _():
        for copy in down:
            copy.wait_send()

    @pl.when(is_top)
    def _():
        for copy in strip_straight:
            copy.wait_send()
        for away, copy, _ in strip_mirrored:
            @pl.when(away)
            def _():
                copy.wait_send()


def balance_kernel(y_ref, elev_ref, k_ref, ratio_ref, sigma_ref, expand_ref, state_ref, height_ref, inverse):
    lon_cells, _, lat_cells = y_ref.shape
    levels = state_ref.shape[2]
    sub = lax.broadcasted_iota(jnp.int32, (8, lat_cells), 0)

    def column(ref):
        result = jnp.zeros((8, lat_cells), F32)
        for c in range(2):
            for level in range(levels):
                result = jnp.where(sub == levels * c + level, ref[c, level], result)
        return result

    sigma, expand = column(sigma_ref), column(expand_ref)
    inverse[...] = 1.0 / k_ref[...]

    def one(i, carry):
        scaled = y_ref[i] * (sigma * jnp.broadcast_to(inverse[pl.ds(i, 1), :], (8, lat_cells)))
        ratio = jnp.broadcast_to(ratio_ref[pl.ds(i, 1), :], (8, lat_cells))
        state = scaled + jnp.where(sub >= levels, ratio * pltpu.roll(scaled, levels, 0), 0.0)
        state_ref[0, i] = state[0:levels]
        state_ref[1, i] = state[levels : 2 * levels]
        height_ref[pl.ds(i, 1), :] = elev_ref[pl.ds(i, 1), :] + jnp.sum(expand * state, axis=0, keepdims=True)
        return carry

    lax.fori_loop(0, lon_cells, one, 0, unroll=17)


def local(
    n_lon, n_lat,
    control_fields,
    unexplained_elevation,
    diffusivity,
    depth_levels,
    fold_partner,
    prior_sigmas,
    haline_thermal_ratio,
    expansion_coefficients,
):
    levels, lon_cells, lat_cells = control_fields.shape[1:]
    fields = jnp.transpose(control_fields, (0, 2, 1, 3))
    rows = lon_cells + 2 * PASSES
    wide = lat_cells + LANES
    vmem = pl.BlockSpec(memory_space=pltpu.VMEM)
    smem = pl.BlockSpec(memory_space=pltpu.SMEM)
    hbm = pl.BlockSpec(memory_space=pltpu.HBM)
    final = pl.pallas_call(
        functools.partial(diffuse_kernel, n_lon, n_lat),
        name="diffuse",
        out_shape=jax.ShapeDtypeStruct((lon_cells, 2 * levels, lat_cells), F32),
        in_specs=[hbm] * 4,
        out_specs=vmem,
        scratch_shapes=[
            pltpu.VMEM(fields.shape, F32),
            pltpu.VMEM((lon_cells, lat_cells), F32),
            pltpu.VMEM((lon_cells, lat_cells), jnp.int32),
            pltpu.SMEM(fold_partner.shape, jnp.int32),
            *[pltpu.VMEM((rows, 8, wide), F32) for _ in range(7)],
            pltpu.VMEM((2, 8, lat_cells), F32),
            pltpu.VMEM((2, 2, 4, levels, lat_cells), F32),
            pltpu.VMEM((2, 8, lat_cells), F32),
            pltpu.VMEM((2, 6, 8, LANES), F32),
            pltpu.VMEM((2, 5, 8, LANES), F32),
            pltpu.VMEM((4, 8, LANES), F32),
            pltpu.VMEM((6, 8, LANES), F32),
            pltpu.VMEM((10, 6, 8, LANES), F32),
            pltpu.SemaphoreType.DMA((8,)),
            pltpu.SemaphoreType.DMA((20,)),
            pltpu.SemaphoreType.DMA((20,)),
        ],
        compiler_params=pltpu.CompilerParams(
            collective_id=0, has_side_effects=True, vmem_limit_bytes=40 * 1024 * 1024
        ),
    )(*[pltpu.with_memory_space_constraint(v, pltpu.HBM) for v in (fields, diffusivity, depth_levels, fold_partner)])
    state, height = pl.pallas_call(
        balance_kernel,
        name="balance",
        out_shape=(
            jax.ShapeDtypeStruct(fields.shape, F32),
            jax.ShapeDtypeStruct((lon_cells, lat_cells), F32),
        ),
        in_specs=[vmem] * 4 + [smem] * 2,
        out_specs=(vmem, vmem),
        scratch_shapes=[pltpu.VMEM((lon_cells, lat_cells), F32)],
        compiler_params=pltpu.CompilerParams(vmem_limit_bytes=40 * 1024 * 1024),
    )(final, unexplained_elevation, diffusivity, haline_thermal_ratio, prior_sigmas, expansion_coefficients)
    return jnp.transpose(state, (0, 2, 1, 3)), height


def solution(mesh):
    return jax.shard_map(
        functools.partial(local, mesh.shape["lon"], mesh.shape["lat"]),
        mesh=mesh,
        in_specs=(
            P(None, None, "lon", "lat"),
            P("lon", "lat"),
            P("lon", "lat"),
            P("lon", "lat"),
            P(),
            P(),
            P("lon", "lat"),
            P(),
        ),
        out_specs=(P(None, None, "lon", "lat"), P("lon", "lat")),
        check_vma=False,
    )
```

```python
import functools

import jax
import jax.numpy as jnp
from jax import lax
from jax.experimental import pallas as pl
from jax.experimental.pallas import tpu as pltpu
from jax.sharding import PartitionSpec as P

PASSES = 4
LANES = 128
SLOT = 16
GROUPS = LANES // SLOT
STRAIGHT_ROWS = (1, 2, 3, 2, 1)
MIRROR_ROWS = (2, 3, 4, 3, 2)
MESH = pl.DeviceIdType.MESH
F32 = jnp.float32


def strip_pieces(rows):
    return rows + (rows + 1) // 2


def iotas():
    shape = (8, LANES)
    return lax.broadcasted_iota(jnp.int32, shape, 1), lax.broadcasted_iota(jnp.int32, shape, 0)


def take(values, index):
    return jnp.take_along_axis(values, index, axis=1, mode="promise_in_bounds")


def roll(values, shift):
    shift = shift % LANES
    return pltpu.roll(values, shift, 1) if shift else values


def make_strip(stride, p_src, q_src):
    lane, sub = iotas()
    row_at = lane + PASSES
    m, g = row_at % stride, row_at // stride

    def row(r, parts):
        index = jnp.minimum(SLOT * g + 4 * (m % 4) + (PASSES - 1 - r), LANES - 1)
        result = take(parts[0], index)
        for n in range(1, len(parts)):
            result = jnp.where(m // 4 == n, take(parts[n], index), result)
        return result

    count = -(-stride // 4)
    fields = [p_src[0, n] for n in range(count)]
    weights = [p_src[0, count + n] for n in range(count)]
    for t in range(2):
        q_src[3 * t] = jnp.where(sub < 4, row(2 * t, weights), row(2 * t + 1, weights))
        for h in range(2):
            q_src[3 * t + 1 + h] = row(2 * t + h, fields)


def fold_blocks(n_lon, b):
    return {
        (kind, o): lax.rem((b if kind == "S" else -b) + o + 2 * n_lon, n_lon) for kind in "SM" for o in range(-2, 3)
    }


def fold_index(n_lon, lon_cells, b, fp_s, fp_v):
    lane, _ = iotas()
    blocks = list(fold_blocks(n_lon, b).values())

    def collect(l, rows):
        return tuple(
            jnp.where(lane == l, fp_s[block * lon_cells + l] - lax.rem(n_lon - block, n_lon) * lon_cells, row)
            for block, row in zip(blocks, rows)
        )

    nothing = jnp.zeros((8, LANES), jnp.int32)
    for n, row in enumerate(lax.fori_loop(0, lon_cells, collect, (nothing,) * len(blocks))):
        fp_v[n] = row


def fold_strip(n_lon, lon_cells, stride, b, q_src, q_land, fp_v, fold_v):
    lane, sub = iotas()
    index = {where: fp_v[n] for n, where in enumerate(fold_blocks(n_lon, b))}
    kinds = {"S": STRAIGHT_ROWS, "M": MIRROR_ROWS}
    y, kw = {}, {}
    for kind, rows in kinds.items():
        for o in range(-2, 3):
            slot = o + 2 + (0 if kind == "S" else 5)
            piece = (lambda i: q_src[i]) if slot == 2 else (lambda i, slot=slot: q_land[slot, i])
            for r in range(rows[o + 2]):
                t, h = r // 2, r % 2
                pair = piece(3 * t)
                turned = pltpu.roll(pair, 4, 0)
                kw[kind, o, r] = jnp.where((sub < 4) if h == 0 else (sub >= 4), pair, turned)
                y[kind, o, r] = piece(3 * t + 1 + h)

    other = {"S": "M", "M": "S"}

    def sides(table, kind, o, r):
        here = table[kind, o, r]
        from_east = table.get((kind, o + 1, r), here)
        from_west = table.get((kind, o - 1, r), here)
        return jnp.where(lane == lon_cells - 1, roll(from_east, lon_cells - 1), roll(here, -1)) + jnp.where(
            lane == 0, roll(from_west, 1 - lon_cells), roll(here, 1)
        )

    def above(table, kind, o, r):
        if r:
            return table[kind, o, r - 1]
        return take(table[other[kind], -o, 0], index[kind, o])

    def around(table, kind, o, r):
        return sides(table, kind, o, r) + above(table, kind, o, r) + table[kind, o, r + 1]

    slots = [jnp.minimum(m + stride * (lane // SLOT), LANES - 1) for m in range(stride)]

    def keep(n, table):
        own = take(table["M", 0, 0], index["S", 0])
        right = take(table["M", -1, 0], index["S", 1])
        left = take(table["M", 1, 0], index["S", -1])
        result = jnp.where(
            lane < 4, roll(left, 4 - lon_cells), jnp.where(lane < 4 + lon_cells, roll(own, 4), roll(right, 4 + lon_cells))
        )
        result = jnp.where(lane < 8 + lon_cells, result, 0.0)
        for m in range(stride):
            fold_v[n, m] = take(result, slots[m])

    keep(PASSES, kw)
    keep(0, y)
    coefficients = {}
    for step in range(1, PASSES):
        renewed = {}
        for kind, rows in kinds.items():
            for o in range(-2, 3):
                for r in range(rows[o + 2] - step):
                    if (kind, o, r) not in coefficients:
                        k0 = kw[kind, o, r]
                        coefficients[kind, o, r] = 1.0 - k0 * around(kw, kind, o, r), k0 * k0
                    c, q = coefficients[kind, o, r]
                    renewed[kind, o, r] = c * y[kind, o, r] + q * around(y, kind, o, r)
        y.update(renewed)
        keep(step, y)


def diffuse_kernel(
    n_lon, n_lat,
    x_hbm, k_hbm, d_hbm, fp_hbm, sigma_hbm, expand_hbm,
    y_out, edge_out, inverse_out, column_out,
    x_v, k_v, d_v, fp_s, sigma_s, expand_s, fp_v,
    y0, y1, y2, y3, kw, cc, qq, edge_y, edge_kw, fold_v,
    kd_src, x_land, kd_land, p_src, p_land, c_land, q_src, q_land,
    local_sem, send_sem, recv_sem,
):
    lon_cells, lat_cells = k_hbm.shape
    rows = lon_cells + 2 * PASSES
    stride = edge_y.shape[1]
    parts = -(-stride // 4)
    tiles = lat_cells // LANES
    b = lax.axis_index("lon")
    a = lax.axis_index("lat")
    has_n = a < n_lat - 1
    has_s = a > 0
    is_top = a == n_lat - 1
    first_lon = b == 0
    east = lax.rem(b + 1, n_lon)
    west = lax.rem(b + n_lon - 1, n_lon)
    north = lax.rem(a + 1, n_lat)
    south = lax.rem(a + n_lat - 1, n_lat)
    lane, sub = iotas()
    spot = lane % SLOT

    straight = [
        (slot, STRAIGHT_ROWS[slot], lax.rem(b - (slot - 2) + n_lon, n_lon)) for slot in (0, 1, 3, 4)
    ]
    mirrored = [
        (5 + slot, MIRROR_ROWS[slot], lax.rem((slot - 2) - b + 2 * n_lon, n_lon)) for slot in range(5)
    ]

    barrier = pltpu.get_barrier_semaphore()

    def hail(lon, lat):
        pl.semaphore_signal(barrier, inc=1, device_id={"lon": lon, "lat": lat}, device_id_type=MESH)

    hail(west, a)
    hail(east, a)

    @pl.when(has_n)
    def _():
        for lon in (b, east, west):
            hail(lon, north)

    @pl.when(has_s)
    def _():
        for lon in (b, east, west):
            hail(lon, south)

    @pl.when(is_top)
    def _():
        for _, _, target in straight:
            hail(target, a)
        for _, _, target in mirrored:
            @pl.when(target != b)
            def _():
                hail(target, a)

    expected = 2 + jnp.where(has_n, 3, 0) + jnp.where(has_s, 3, 0) + jnp.where(is_top, 4, 0)
    for _, _, target in mirrored:
        expected = expected + jnp.where(jnp.logical_and(is_top, target != b), 1, 0)

    chunk = 17
    load_k = pltpu.make_async_copy(k_hbm, k_v, local_sem.at[0])
    load_d = pltpu.make_async_copy(d_hbm, d_v, local_sem.at[1])
    small = [
        pltpu.make_async_copy(fp_hbm, fp_s, local_sem.at[2]),
        pltpu.make_async_copy(sigma_hbm, sigma_s, local_sem.at[3]),
        pltpu.make_async_copy(expand_hbm, expand_s, local_sem.at[4]),
    ]
    loads = [
        pltpu.make_async_copy(
            x_hbm.at[:, pl.ds(chunk * n, chunk)], x_v.at[:, pl.ds(chunk * n, chunk)], local_sem.at[5 + n]
        )
        for n in range(lon_cells // chunk)
    ]
    for copy in [load_k, load_d, *loads, *small]:
        copy.start()

    def remote(src, dst, index, lon, lat):
        return pltpu.make_async_remote_copy(
            src_ref=src, dst_ref=dst, send_sem=send_sem.at[index], recv_sem=recv_sem.at[index],
            device_id={"lon": lon, "lat": lat}, device_id_type=MESH,
        )

    along = [
        remote(x_hbm.at[:, pl.ds(lon_cells - 4, 4)], x_land.at[0], 0, east, a),
        remote(x_hbm.at[:, pl.ds(0, 4)], x_land.at[1], 1, west, a),
        remote(kd_src.at[0], kd_land.at[0], 2, east, a),
        remote(kd_src.at[1], kd_land.at[1], 3, west, a),
    ]
    whole = pl.ds(0, 2 * parts)
    up = [
        remote(p_src.at[0, whole], p_land.at[0], 4, b, north),
        remote(p_src.at[0, 2 * parts], c_land.at[0], 6, east, north),
        remote(p_src.at[0, 2 * parts + 1], c_land.at[1], 7, west, north),
    ]
    down = [
        remote(p_src.at[1, whole], p_land.at[1], 5, b, south),
        remote(p_src.at[1, 2 * parts], c_land.at[2], 8, east, south),
        remote(p_src.at[1, 2 * parts + 1], c_land.at[3], 9, west, south),
    ]

    def strip(slot, count, target):
        part = pl.ds(0, strip_pieces(count))
        return remote(q_src.at[part], q_land.at[slot, part], 10 + slot, target, a)

    strip_straight = [strip(*which) for which in straight]
    strip_mirrored = [(which[2] != b, strip(*which), which[0]) for which in mirrored]

    load_k.wait()
    load_d.wait()
    kd_src[0, 0:4] = k_v[lon_cells - 4 : lon_cells, :]
    kd_src[0, 4:8] = d_v[lon_cells - 4 : lon_cells, :].astype(F32)
    kd_src[1, 0:4] = k_v[0:4, :]
    kd_src[1, 4:8] = d_v[0:4, :].astype(F32)

    def send_along():
        pl.semaphore_wait(barrier, expected)
        for copy in along:
            copy.start()

    def send_edges():
        @pl.when(has_n)
        def _():
            for copy in up:
                copy.start()

        @pl.when(has_s)
        def _():
            for copy in down:
                copy.start()

        @pl.when(is_top)
        def _():
            for copy in strip_straight:
                copy.start()
            for away, copy, _ in strip_mirrored:
                @pl.when(away)
                def _():
                    copy.start()

    @pl.when(jnp.logical_not(first_lon))
    def _():
        send_along()

    wide_level = lax.broadcasted_iota(jnp.int32, (8, lat_cells), 0) % 4

    def own_weights(i, carry):
        k = jnp.broadcast_to(k_v[pl.ds(i, 1), :], (8, lat_cells))
        d = jnp.broadcast_to(d_v[pl.ds(i, 1), :], (8, lat_cells))
        kw[i + PASSES] = jnp.where(d > wide_level, k, 0.0)
        return carry

    lax.fori_loop(0, lon_cells, own_weights, 0, unroll=17)
    for copy in loads:
        copy.wait()

    def own_fields(i, carry):
        x = jnp.concatenate([x_v[0, i], x_v[1, i]], axis=0)
        y0[i + PASSES] = x * kw[i + PASSES]
        return carry

    lax.fori_loop(0, lon_cells, own_fields, 0, unroll=17)

    def outer(ref, side, row):
        g = row // stride
        if side == 0:
            return roll(ref[row, :, lat_cells - LANES : lat_cells], SLOT * g + 8)
        return roll(ref[row, :, 0:LANES], SLOT * g + 4)

    inside = [spot < 8, jnp.logical_and(spot >= 4, spot < 12)]
    places = ((y0, edge_y), (kw, edge_kw))
    for side in range(2):
        for which, (ref, edge) in enumerate(places):
            pieces = []
            for m in range(stride):
                piece = jnp.zeros((8, LANES), F32)
                for g in range(GROUPS):
                    row = m + stride * g
                    if PASSES <= row < rows - PASSES:
                        piece = jnp.where(lane >= SLOT * g, outer(ref, side, row), piece)
                    elif row >= rows - PASSES:
                        piece = jnp.where(lane >= SLOT * g, 0.0, piece)
                piece = jnp.where(inside[side], piece, 0.0)
                edge[side, m] = piece
                pieces.append(piece)
            for n in range(parts):
                packed = jnp.zeros((8, LANES), F32)
                for t in range(4):
                    if 4 * n + t < stride:
                        packed = jnp.where(spot // 4 == t, roll(pieces[4 * n + t], 4 * t - 4), packed)
                p_src[side, parts * which + n] = packed
            for end, start in ((0, rows - 2 * PASSES), (1, PASSES)):
                corner = jnp.zeros((8, LANES), F32) if which == 0 else p_src[side, 2 * parts + end]
                for r in range(4):
                    m, g = (start + r) % stride, (start + r) // stride
                    at = 4 * (r + 4 * which)
                    corner = jnp.where(
                        jnp.logical_and(lane >= at, lane < at + 4), roll(pieces[m], at - SLOT * g - 4), corner
                    )
                p_src[side, 2 * parts + end] = corner

    @pl.when(is_top)
    def _():
        make_strip(stride, p_src, q_src)
        for away, _, slot in strip_mirrored:
            @pl.when(jnp.logical_not(away))
            def _():
                q_land[slot] = q_src[...]

    @pl.when(jnp.logical_not(first_lon))
    def _():
        send_edges()

    for copy in small:
        copy.wait()

    @pl.when(is_top)
    def _():
        fold_index(n_lon, lon_cells, b, fp_s, fp_v)

    for n, ref in enumerate((sigma_s, expand_s)):
        column = jnp.zeros((8, LANES), F32)
        for c in range(2):
            for level in range(4):
                column = jnp.where(sub == 4 * c + level, ref[c, level], column)
        column_out[n] = column
    inverse_out[...] = 1.0 / k_v[...]

    def lattice(ref, row):
        here = [ref[row, :, LANES * t : LANES * (t + 1)] for t in range(tiles)]
        up_one = [roll(v, -1) for v in here]
        down_one = [roll(v, 1) for v in here]
        sums = []
        for t in range(tiles):
            n = jnp.where(lane == LANES - 1, up_one[(t + 1) % tiles], up_one[t])
            s = jnp.where(lane == 0, down_one[t - 1], down_one[t])
            at = slice(LANES * t, LANES * (t + 1))
            sums.append((n + s) + (ref[row + 1, :, at] + ref[row - 1, :, at]))
        return here, sums

    def coefficients(row):
        here, sums = lattice(kw, row)
        for t in range(tiles):
            cc[row, :, LANES * t : LANES * (t + 1)] = 1.0 - here[t] * sums[t]
            qq[row, :, LANES * t : LANES * (t + 1)] = here[t] * here[t]

    states = [y0, y1, y2, y3]

    def advance(step, row):
        here, sums = lattice(states[step], row)
        for t in range(tiles):
            at = slice(LANES * t, LANES * (t + 1))
            new = cc[row, :, at] * here[t] + qq[row, :, at] * sums[t]
            if step < PASSES - 1:
                states[step + 1][row, :, at] = new
            else:
                y_out[row - PASSES, :, at] = new

    def over_rows(first, last, body, unroll):
        def one(row, carry):
            body(row)
            return carry

        lax.fori_loop(first, last, one, 0, unroll=unroll)

    over_rows(PASSES + 1, rows - PASSES - 1, coefficients, 33)
    for step in range(PASSES):
        over_rows(PASSES + 1 + step, rows - PASSES - 1 - step, functools.partial(advance, step), 33 - step)

    @pl.when(first_lon)
    def _():
        send_along()
        send_edges()

    @pl.when(has_s)
    def _():
        for copy in up:
            copy.wait_recv()

    @pl.when(jnp.logical_not(has_s))
    def _():
        p_land[0] = jnp.zeros(p_land.shape[1:], F32)
        for n in range(2):
            c_land[n] = jnp.zeros((8, LANES), F32)

    @pl.when(has_n)
    def _():
        for copy in down:
            copy.wait_recv()

    @pl.when(is_top)
    def _():
        p_land[1] = jnp.zeros(p_land.shape[1:], F32)
        for n in range(2, 4):
            c_land[n] = jnp.zeros((8, LANES), F32)
        for copy in strip_straight:
            copy.wait_recv()
        for away, copy, _ in strip_mirrored:
            @pl.when(away)
            def _():
                copy.wait_recv()
        fold_strip(n_lon, lon_cells, stride, b, q_src, q_land, fp_v, fold_v)

    @pl.when(jnp.logical_not(is_top))
    def _():
        fold_v[...] = jnp.zeros(fold_v.shape, F32)

    for copy in along:
        copy.wait_recv()

    for side, row in ((0, 0), (1, rows - PASSES)):
        for g in range(4):
            k = jnp.broadcast_to(kd_land[side, g : g + 1, :], (8, lat_cells))
            d = jnp.broadcast_to(kd_land[side, 4 + g : 5 + g, :], (8, lat_cells))
            w = jnp.where(d > wide_level.astype(F32), k, 0.0)
            kw[row + g] = w
            x = jnp.concatenate([x_land[side, 0, g], x_land[side, 1, g]], axis=0)
            y0[row + g] = x * w

    beyond = [spot < 4, jnp.logical_and(spot >= 8, spot < 12)]
    folded = jnp.logical_and(spot == 8, lane < jnp.where(is_top, LANES, 0))

    def edge_pieces(which, side):
        ref, edge = places[which]
        pieces = []
        for m in range(stride):
            packed = p_land[side, parts * which + m // 4]
            moved = roll(packed, (0 if side == 0 else 8) - 4 * (m % 4))
            pieces.append(jnp.where(beyond[side], moved, edge[1 - side, m]))
        for end, start in ((0, 0), (1, rows - PASSES)):
            corner = c_land[2 * side + end]
            for r in range(4):
                m, g = (start + r) % stride, (start + r) // stride
                at = 4 * (r + 4 * which)
                ghost = roll(corner, (0 if side == 0 else 8) + SLOT * g - at)
                own = jnp.where(inside[1 - side], outer(ref, 1 - side, start + r), 0.0)
                both = jnp.where(beyond[side], ghost, own)
                pieces[m] = jnp.where(lane // SLOT == g, both, pieces[m])
        return pieces

    def edge_sums(pieces):
        sums = []
        for m in range(stride):
            e = pieces[m + 1] if m < stride - 1 else roll(pieces[0], -SLOT)
            w = pieces[m - 1] if m else roll(pieces[stride - 1], SLOT)
            sums.append((roll(pieces[m], -1) + roll(pieces[m], 1)) + (e + w))
        return sums

    def at_fold(step, pieces, side):
        if side == 0:
            return pieces
        return [jnp.where(folded, fold_v[step, m], pieces[m]) for m in range(stride)]

    edges, edge_c, edge_q = [], [], []
    for side in range(2):
        weights = at_fold(PASSES, edge_pieces(1, side), side)
        edge_c.append([1.0 - w * total for w, total in zip(weights, edge_sums(weights))])
        edge_q.append([w * w for w in weights])
        edges.append(edge_pieces(0, side))
    for n in range(PASSES):
        coefficients(1 + n)
        coefficients(rows - 2 - n)
    for step in range(PASSES):
        for side in range(2):
            pieces = at_fold(step, edges[side], side)
            edges[side] = [
                c * y + q * total
                for c, y, q, total in zip(edge_c[side], pieces, edge_q[side], edge_sums(pieces))
            ]
        for n in range(PASSES):
            advance(step, 1 + step + n)
            advance(step, rows - 2 - step - n)
    for side in range(2):
        for m in range(stride):
            edge_out[side, m] = edges[side][m]

    for copy in along:
        copy.wait_send()

    @pl.when(has_n)
    def _():
        for copy in up:
            copy.wait_send()

    @pl.when(has_s)
    def _():
        for copy in down:
            copy.wait_send()

    @pl.when(is_top)
    def _():
        for copy in strip_straight:
            copy.wait_send()
        for away, copy, _ in strip_mirrored:
            @pl.when(away)
            def _():
                copy.wait_send()


def balance_kernel(
    y_ref, edge_ref, inverse_ref, column_ref, elev_ref, ratio_ref,
    state_hbm, height_hbm, state_v, whole_v, height_v, sem,
):
    lon_cells, _, lat_cells = y_ref.shape
    stride = edge_ref.shape[1]
    tiles = lat_cells // LANES
    lane, sub = iotas()
    sigma = column_ref[0]
    expand = [jnp.broadcast_to(column_ref[1, s : s + 1, :], (8, LANES)) for s in range(8)]
    copies = []

    def send(src, dst):
        copies.append(pltpu.make_async_copy(src, dst, sem.at[len(copies)]))
        copies[-1].start()

    def balance(i):
        m, g = (i + PASSES) % stride, (i + PASSES) // stride
        for t in range(tiles):
            at = slice(LANES * t, LANES * (t + 1))
            y = y_ref[i, :, at]
            if t == 0:
                y = jnp.where(lane < 4, roll(edge_ref[0, m], -SLOT * g - 4), y)
            if t == tiles - 1:
                y = jnp.where(lane >= LANES - 4, roll(edge_ref[1, m], LANES - 8 - SLOT * g), y)
            scaled = y * (sigma * jnp.broadcast_to(inverse_ref[i : i + 1, at], (8, LANES)))
            ratio = jnp.broadcast_to(ratio_ref[i : i + 1, at], (8, LANES))
            state = scaled + jnp.where(sub >= 4, ratio * pltpu.roll(scaled, 4, 0), 0.0)
            state_v[0, i, :, at] = state[0:4]
            state_v[1, i, :, at] = state[4:8]
            whole_v[t, 8 * i : 8 * i + 8, :] = state

    done = 0
    for start in range(0, lon_cells, 8):
        count = min(8, lon_cells - start)
        for i in range(start, start + count):
            balance(i)
        for t in range(tiles):
            at = slice(LANES * t, LANES * (t + 1))
            height = elev_ref[start : start + count, at]
            for s in range(8):
                height = height + expand[s][0:count] * whole_v[t, pl.ds(8 * start + s, count, stride=8), :]
            height_v[start : start + count, at] = height
        if start + count - done >= 24 or start + count == lon_cells:
            part = pl.ds(done, start + count - done)
            send(state_v.at[:, part], state_hbm.at[:, part])
            done = start + count
    send(height_v, height_hbm)
    for copy in copies:
        copy.wait()


def local(
    n_lon, n_lat,
    control_fields,
    unexplained_elevation,
    diffusivity,
    depth_levels,
    fold_partner,
    prior_sigmas,
    haline_thermal_ratio,
    expansion_coefficients,
):
    levels, lon_cells, lat_cells = control_fields.shape[1:]
    fields = jnp.transpose(control_fields, (0, 2, 1, 3))
    stacked = 2 * levels
    rows = lon_cells + 2 * PASSES
    stride = -(-rows // GROUPS)
    parts = -(-stride // 4)
    vmem = pl.BlockSpec(memory_space=pltpu.VMEM)
    hbm = pl.BlockSpec(memory_space=pltpu.HBM)

    def shape(*dims):
        return jax.ShapeDtypeStruct(dims, F32)

    def tile(*dims):
        return pltpu.VMEM((*dims, 8, LANES), F32)

    def in_hbm(*arrays):
        return [pltpu.with_memory_space_constraint(array, pltpu.HBM) for array in arrays]

    passed = pl.pallas_call(
        functools.partial(diffuse_kernel, n_lon, n_lat),
        name="diffuse",
        out_shape=(
            shape(lon_cells, stacked, lat_cells),
            shape(2, stride, 8, LANES),
            shape(lon_cells, lat_cells),
            shape(2, 8, LANES),
        ),
        in_specs=[hbm] * 6,
        out_specs=(vmem,) * 4,
        scratch_shapes=[
            pltpu.VMEM(fields.shape, F32),
            pltpu.VMEM((lon_cells, lat_cells), F32),
            pltpu.VMEM((lon_cells, lat_cells), jnp.int32),
            pltpu.SMEM(fold_partner.shape, jnp.int32),
            pltpu.SMEM(prior_sigmas.shape, F32),
            pltpu.SMEM(expansion_coefficients.shape, F32),
            pltpu.VMEM((10, 8, LANES), jnp.int32),
            *[pltpu.VMEM((rows, 8, lat_cells), F32) for _ in range(7)],
            tile(2, stride),
            tile(2, stride),
            tile(PASSES + 1, stride),
            pltpu.VMEM((2, 8, lat_cells), F32),
            pltpu.VMEM((2, 2, 4, levels, lat_cells), F32),
            pltpu.VMEM((2, 8, lat_cells), F32),
            tile(2, 2 * parts + 2),
            tile(2, 2 * parts),
            tile(4),
            tile(6),
            tile(10, 6),
            pltpu.SemaphoreType.DMA((9,)),
            pltpu.SemaphoreType.DMA((20,)),
            pltpu.SemaphoreType.DMA((20,)),
        ],
        compiler_params=pltpu.CompilerParams(
            collective_id=0, has_side_effects=True, vmem_limit_bytes=40 * 1024 * 1024
        ),
    )(*in_hbm(fields, diffusivity, depth_levels, fold_partner, prior_sigmas, expansion_coefficients))
    state, height = pl.pallas_call(
        balance_kernel,
        name="balance",
        out_shape=(shape(*fields.shape), shape(lon_cells, lat_cells)),
        in_specs=[vmem] * 6,
        out_specs=(hbm, hbm),
        scratch_shapes=[
            pltpu.VMEM(fields.shape, F32),
            pltpu.VMEM((lat_cells // LANES, 8 * lon_cells, LANES), F32),
            pltpu.VMEM((lon_cells, lat_cells), F32),
            pltpu.SemaphoreType.DMA((8,)),
        ],
        compiler_params=pltpu.CompilerParams(vmem_limit_bytes=40 * 1024 * 1024),
    )(*passed, unexplained_elevation, haline_thermal_ratio)
    return jnp.transpose(state, (0, 2, 1, 3)), height


def solution(mesh):
    return jax.shard_map(
        functools.partial(local, mesh.shape["lon"], mesh.shape["lat"]),
        mesh=mesh,
        in_specs=(
            P(None, None, "lon", "lat"),
            P("lon", "lat"),
            P("lon", "lat"),
            P("lon", "lat"),
            P(),
            P(),
            P("lon", "lat"),
            P(),
        ),
        out_specs=(P(None, None, "lon", "lat"), P("lon", "lat")),
        check_vma=False,
    )
```

```python
import functools

import jax
import jax.numpy as jnp
from jax import lax
from jax.experimental import pallas as pl
from jax.experimental.pallas import tpu as pltpu
from jax.sharding import PartitionSpec as P

PASSES = 4
LANES = 128
SLOT = 16
GROUPS = LANES // SLOT
STRAIGHT_ROWS = (1, 2, 3, 2, 1)
MIRROR_ROWS = (2, 3, 4, 3, 2)
MESH = pl.DeviceIdType.MESH
F32 = jnp.float32


def strip_pieces(rows):
    return rows + (rows + 1) // 2


def iotas():
    shape = (8, LANES)
    return lax.broadcasted_iota(jnp.int32, shape, 1), lax.broadcasted_iota(jnp.int32, shape, 0)


def take(values, index):
    return jnp.take_along_axis(values, index, axis=1, mode="promise_in_bounds")


def roll(values, shift):
    shift = shift % LANES
    return pltpu.roll(values, shift, 1) if shift else values


def make_strip(stride, p_src, q_src):
    lane, sub = iotas()
    row_at = lane + PASSES
    m, g = row_at % stride, row_at // stride

    def row(r, parts):
        index = jnp.minimum(SLOT * g + 4 * (m % 4) + (PASSES - 1 - r), LANES - 1)
        result = take(parts[0], index)
        for n in range(1, len(parts)):
            result = jnp.where(m // 4 == n, take(parts[n], index), result)
        return result

    count = -(-stride // 4)
    fields = [p_src[0, n] for n in range(count)]
    weights = [p_src[0, count + n] for n in range(count)]
    for t in range(2):
        q_src[3 * t] = jnp.where(sub < 4, row(2 * t, weights), row(2 * t + 1, weights))
        for h in range(2):
            q_src[3 * t + 1 + h] = row(2 * t + h, fields)


def fold_blocks(n_lon, b):
    return {
        (kind, o): lax.rem((b if kind == "S" else -b) + o + 2 * n_lon, n_lon) for kind in "SM" for o in range(-2, 3)
    }


def fold_index(n_lon, lon_cells, b, fp_s, fp_v):
    lane, _ = iotas()
    blocks = list(fold_blocks(n_lon, b).values())

    def collect(l, rows):
        return tuple(
            jnp.where(lane == l, fp_s[block * lon_cells + l] - lax.rem(n_lon - block, n_lon) * lon_cells, row)
            for block, row in zip(blocks, rows)
        )

    nothing = jnp.zeros((8, LANES), jnp.int32)
    for n, row in enumerate(lax.fori_loop(0, lon_cells, collect, (nothing,) * len(blocks), unroll=4)):
        fp_v[n] = row


def fold_strip(n_lon, lon_cells, stride, b, q_src, q_land, fp_v, fold_v):
    lane, sub = iotas()
    index = {where: fp_v[n] for n, where in enumerate(fold_blocks(n_lon, b))}
    kinds = {"S": STRAIGHT_ROWS, "M": MIRROR_ROWS}
    y, kw = {}, {}
    for kind, rows in kinds.items():
        for o in range(-2, 3):
            slot = o + 2 + (0 if kind == "S" else 5)
            piece = (lambda i: q_src[i]) if slot == 2 else (lambda i, slot=slot: q_land[slot, i])
            for r in range(rows[o + 2]):
                t, h = r // 2, r % 2
                pair = piece(3 * t)
                turned = pltpu.roll(pair, 4, 0)
                kw[kind, o, r] = jnp.where((sub < 4) if h == 0 else (sub >= 4), pair, turned)
                y[kind, o, r] = piece(3 * t + 1 + h)

    other = {"S": "M", "M": "S"}

    def sides(table, kind, o, r):
        here = table[kind, o, r]
        from_east = table.get((kind, o + 1, r), here)
        from_west = table.get((kind, o - 1, r), here)
        return jnp.where(lane == lon_cells - 1, roll(from_east, lon_cells - 1), roll(here, -1)) + jnp.where(
            lane == 0, roll(from_west, 1 - lon_cells), roll(here, 1)
        )

    def above(table, kind, o, r):
        if r:
            return table[kind, o, r - 1]
        return take(table[other[kind], -o, 0], index[kind, o])

    def around(table, kind, o, r):
        return sides(table, kind, o, r) + above(table, kind, o, r) + table[kind, o, r + 1]

    slots = [jnp.minimum(m + stride * (lane // SLOT), LANES - 1) for m in range(stride)]

    def keep(n, table):
        own = take(table["M", 0, 0], index["S", 0])
        right = take(table["M", -1, 0], index["S", 1])
        left = take(table["M", 1, 0], index["S", -1])
        result = jnp.where(
            lane < 4, roll(left, 4 - lon_cells), jnp.where(lane < 4 + lon_cells, roll(own, 4), roll(right, 4 + lon_cells))
        )
        result = jnp.where(lane < 8 + lon_cells, result, 0.0)
        for m in range(stride):
            fold_v[n, m] = take(result, slots[m])

    keep(PASSES, kw)
    keep(0, y)
    coefficients = {}
    for step in range(1, PASSES):
        renewed = {}
        for kind, rows in kinds.items():
            for o in range(-2, 3):
                for r in range(rows[o + 2] - step):
                    if (kind, o, r) not in coefficients:
                        k0 = kw[kind, o, r]
                        coefficients[kind, o, r] = 1.0 - k0 * around(kw, kind, o, r), k0 * k0
                    c, q = coefficients[kind, o, r]
                    renewed[kind, o, r] = c * y[kind, o, r] + q * around(y, kind, o, r)
        y.update(renewed)
        keep(step, y)


def diffuse_kernel(
    n_lon, n_lat,
    x_hbm, k_hbm, d_hbm, fp_hbm, sigma_hbm, expand_hbm,
    y_out, edge_out, inverse_out, column_out,
    x_v, k_v, d_v, fp_s, sigma_s, expand_s, fp_v,
    y0, y1, y2, y3, kw, cc, qq, edge_y, edge_kw, fold_v,
    kd_src, x_land, kd_land, p_src, p_land, c_land, q_src, q_land,
    local_sem, send_sem, recv_sem,
):
    lon_cells, lat_cells = k_hbm.shape
    rows = lon_cells + 2 * PASSES
    stride = edge_y.shape[1]
    parts = -(-stride // 4)
    tiles = lat_cells // LANES
    b = lax.axis_index("lon")
    a = lax.axis_index("lat")
    has_n = a < n_lat - 1
    has_s = a > 0
    is_top = a == n_lat - 1
    first_lon = b == 0
    east = lax.rem(b + 1, n_lon)
    west = lax.rem(b + n_lon - 1, n_lon)
    north = lax.rem(a + 1, n_lat)
    south = lax.rem(a + n_lat - 1, n_lat)
    lane, sub = iotas()
    spot = lane % SLOT

    straight = [
        (slot, STRAIGHT_ROWS[slot], lax.rem(b - (slot - 2) + n_lon, n_lon)) for slot in (0, 1, 3, 4)
    ]
    mirrored = [
        (5 + slot, MIRROR_ROWS[slot], lax.rem((slot - 2) - b + 2 * n_lon, n_lon)) for slot in range(5)
    ]

    barrier = pltpu.get_barrier_semaphore()

    def hail(lon, lat):
        pl.semaphore_signal(barrier, inc=1, device_id={"lon": lon, "lat": lat}, device_id_type=MESH)

    hail(west, a)
    hail(east, a)

    @pl.when(has_n)
    def _():
        for lon in (b, east, west):
            hail(lon, north)

    @pl.when(has_s)
    def _():
        for lon in (b, east, west):
            hail(lon, south)

    @pl.when(is_top)
    def _():
        for _, _, target in straight:
            hail(target, a)
        for _, _, target in mirrored:
            @pl.when(target != b)
            def _():
                hail(target, a)

    expected = 2 + jnp.where(has_n, 3, 0) + jnp.where(has_s, 3, 0) + jnp.where(is_top, 4, 0)
    for _, _, target in mirrored:
        expected = expected + jnp.where(jnp.logical_and(is_top, target != b), 1, 0)

    chunk = 17
    load_k = pltpu.make_async_copy(k_hbm, k_v, local_sem.at[0])
    load_d = pltpu.make_async_copy(d_hbm, d_v, local_sem.at[1])
    small = [
        pltpu.make_async_copy(fp_hbm, fp_s, local_sem.at[2]),
        pltpu.make_async_copy(sigma_hbm, sigma_s, local_sem.at[3]),
        pltpu.make_async_copy(expand_hbm, expand_s, local_sem.at[4]),
    ]
    loads = [
        pltpu.make_async_copy(
            x_hbm.at[:, pl.ds(chunk * n, chunk)], x_v.at[:, pl.ds(chunk * n, chunk)], local_sem.at[5 + n]
        )
        for n in range(lon_cells // chunk)
    ]
    for copy in [load_k, load_d, loads[0], loads[-1], *loads[1:-1], *small]:
        copy.start()

    def remote(src, dst, index, lon, lat):
        return pltpu.make_async_remote_copy(
            src_ref=src, dst_ref=dst, send_sem=send_sem.at[index], recv_sem=recv_sem.at[index],
            device_id={"lon": lon, "lat": lat}, device_id_type=MESH,
        )

    along = [
        remote(x_hbm.at[:, pl.ds(lon_cells - 4, 4)], x_land.at[0], 0, east, a),
        remote(x_hbm.at[:, pl.ds(0, 4)], x_land.at[1], 1, west, a),
        remote(kd_src.at[0], kd_land.at[0], 2, east, a),
        remote(kd_src.at[1], kd_land.at[1], 3, west, a),
    ]
    whole = pl.ds(0, 2 * parts)
    up = [
        remote(p_src.at[0, whole], p_land.at[0], 4, b, north),
        remote(p_src.at[0, 2 * parts], c_land.at[0], 6, east, north),
        remote(p_src.at[0, 2 * parts + 1], c_land.at[1], 7, west, north),
    ]
    down = [
        remote(p_src.at[1, whole], p_land.at[1], 5, b, south),
        remote(p_src.at[1, 2 * parts], c_land.at[2], 8, east, south),
        remote(p_src.at[1, 2 * parts + 1], c_land.at[3], 9, west, south),
    ]

    def strip(slot, count, target):
        part = pl.ds(0, strip_pieces(count))
        return remote(q_src.at[part], q_land.at[slot, part], 10 + slot, target, a)

    strip_straight = [strip(*which) for which in straight]
    strip_mirrored = [(which[2] != b, strip(*which), which[0]) for which in mirrored]

    def send_fields():
        for copy in along[:2]:
            copy.start()

    def send_weights():
        for copy in along[2:]:
            copy.start()

    def send_corners():
        @pl.when(has_n)
        def _():
            for copy in up[1:]:
                copy.start()

        @pl.when(has_s)
        def _():
            for copy in down[1:]:
                copy.start()

    def send_edges():
        @pl.when(has_n)
        def _():
            up[0].start()

        @pl.when(has_s)
        def _():
            down[0].start()

    at_once = jnp.logical_not(jnp.logical_or(first_lon, jnp.logical_and(is_top, b < n_lon - 1)))
    last = jnp.logical_and(first_lon, jnp.logical_not(is_top))

    @pl.when(at_once)
    def _():
        pl.semaphore_wait(barrier, expected)
        send_fields()

    load_k.wait()
    load_d.wait()
    kd_src[0, 0:4] = k_v[lon_cells - 4 : lon_cells, :]
    kd_src[0, 4:8] = d_v[lon_cells - 4 : lon_cells, :].astype(F32)
    kd_src[1, 0:4] = k_v[0:4, :]
    kd_src[1, 4:8] = d_v[0:4, :].astype(F32)

    pl.when(at_once)(send_weights)

    loads[0].wait()
    loads[-1].wait()
    level = sub % 4
    wide_level = lax.broadcasted_iota(jnp.int32, (8, lat_cells), 0) % 4

    for side in range(2):
        tile = slice(lat_cells - LANES, lat_cells) if side == 0 else slice(0, LANES)
        for end, start in ((0, lon_cells - 4), (1, 0)):
            corner = jnp.zeros((8, LANES), F32)
            for r in range(4):
                i = start + r
                k = jnp.broadcast_to(k_v[i : i + 1, tile], (8, LANES))
                d = jnp.broadcast_to(d_v[i : i + 1, tile], (8, LANES))
                weight = jnp.where(d > level, k, 0.0)
                field = jnp.concatenate([x_v[0, i, :, tile], x_v[1, i, :, tile]], axis=0) * weight
                for at, value in ((4 * r, field), (4 * (r + 4), weight)):
                    moved = roll(value, at + (4 if side == 0 else 0))
                    corner = jnp.where(jnp.logical_and(lane >= at, lane < at + 4), moved, corner)
            p_src[side, 2 * parts + end] = corner

    pl.when(at_once)(send_corners)

    def own_weights(i, carry):
        k = jnp.broadcast_to(k_v[pl.ds(i, 1), :], (8, lat_cells))
        d = jnp.broadcast_to(d_v[pl.ds(i, 1), :], (8, lat_cells))
        kw[i + PASSES] = jnp.where(d > wide_level, k, 0.0)
        return carry

    lax.fori_loop(0, lon_cells, own_weights, 0, unroll=17)
    for copy in loads[1:-1]:
        copy.wait()

    def own_fields(i, carry):
        x = jnp.concatenate([x_v[0, i], x_v[1, i]], axis=0)
        y0[i + PASSES] = x * kw[i + PASSES]
        return carry

    lax.fori_loop(0, lon_cells, own_fields, 0, unroll=17)

    def outer(ref, side, row):
        g = row // stride
        if side == 0:
            return roll(ref[row, :, lat_cells - LANES : lat_cells], SLOT * g + 8)
        return roll(ref[row, :, 0:LANES], SLOT * g + 4)

    inside = [spot < 8, jnp.logical_and(spot >= 4, spot < 12)]
    places = ((y0, edge_y), (kw, edge_kw))
    for side in range(2):
        for which, (ref, edge) in enumerate(places):
            pieces = []
            for m in range(stride):
                piece = jnp.zeros((8, LANES), F32)
                for g in range(GROUPS):
                    row = m + stride * g
                    if PASSES <= row < rows - PASSES:
                        piece = jnp.where(lane >= SLOT * g, outer(ref, side, row), piece)
                    elif row >= rows - PASSES:
                        piece = jnp.where(lane >= SLOT * g, 0.0, piece)
                piece = jnp.where(inside[side], piece, 0.0)
                edge[side, m] = piece
                pieces.append(piece)
            for n in range(parts):
                packed = jnp.zeros((8, LANES), F32)
                for t in range(4):
                    if 4 * n + t < stride:
                        packed = jnp.where(spot // 4 == t, roll(pieces[4 * n + t], 4 * t - 4), packed)
                p_src[side, parts * which + n] = packed

    pl.when(jnp.logical_and(at_once, jnp.logical_not(is_top)))(send_edges)

    @pl.when(is_top)
    def _():
        make_strip(stride, p_src, q_src)
        @pl.when(jnp.logical_not(at_once))
        def _():
            pl.semaphore_wait(barrier, expected)

        for copy in strip_straight:
            copy.start()
        for away, copy, slot in strip_mirrored:
            @pl.when(away)
            def _():
                copy.start()

            @pl.when(jnp.logical_not(away))
            def _():
                q_land[slot] = q_src[...]
        send_edges()

        @pl.when(jnp.logical_not(at_once))
        def _():
            send_corners()
            send_fields()
            send_weights()

    for copy in small:
        copy.wait()

    @pl.when(is_top)
    def _():
        fold_index(n_lon, lon_cells, b, fp_s, fp_v)

    for n, ref in enumerate((sigma_s, expand_s)):
        column = jnp.zeros((8, LANES), F32)
        for c in range(2):
            for level in range(4):
                column = jnp.where(sub == 4 * c + level, ref[c, level], column)
        column_out[n] = column
    inverse_out[...] = 1.0 / k_v[...]

    def lattice(ref, row):
        here = [ref[row, :, LANES * t : LANES * (t + 1)] for t in range(tiles)]
        up_one = [roll(v, -1) for v in here]
        down_one = [roll(v, 1) for v in here]
        sums = []
        for t in range(tiles):
            n = jnp.where(lane == LANES - 1, up_one[(t + 1) % tiles], up_one[t])
            s = jnp.where(lane == 0, down_one[t - 1], down_one[t])
            at = slice(LANES * t, LANES * (t + 1))
            sums.append((n + s) + (ref[row + 1, :, at] + ref[row - 1, :, at]))
        return here, sums

    def coefficients(row):
        here, sums = lattice(kw, row)
        for t in range(tiles):
            cc[row, :, LANES * t : LANES * (t + 1)] = 1.0 - here[t] * sums[t]
            qq[row, :, LANES * t : LANES * (t + 1)] = here[t] * here[t]

    states = [y0, y1, y2, y3]

    def advance(step, row):
        here, sums = lattice(states[step], row)
        for t in range(tiles):
            at = slice(LANES * t, LANES * (t + 1))
            new = cc[row, :, at] * here[t] + qq[row, :, at] * sums[t]
            if step < PASSES - 1:
                states[step + 1][row, :, at] = new
            else:
                y_out[row - PASSES, :, at] = new

    def over_rows(first, last, body, unroll):
        def one(row, carry):
            body(row)
            return carry

        lax.fori_loop(first, last, one, 0, unroll=unroll)

    over_rows(PASSES + 1, rows - PASSES - 1, coefficients, 33)
    for step in range(PASSES):
        over_rows(PASSES + 1 + step, rows - PASSES - 1 - step, functools.partial(advance, step), 33 - step)

    @pl.when(last)
    def _():
        pl.semaphore_wait(barrier, expected)
        send_fields()
        send_weights()
        send_corners()
        send_edges()

    @pl.when(has_s)
    def _():
        for copy in up:
            copy.wait_recv()

    @pl.when(jnp.logical_not(has_s))
    def _():
        p_land[0] = jnp.zeros(p_land.shape[1:], F32)
        for n in range(2):
            c_land[n] = jnp.zeros((8, LANES), F32)

    @pl.when(has_n)
    def _():
        for copy in down:
            copy.wait_recv()

    @pl.when(is_top)
    def _():
        p_land[1] = jnp.zeros(p_land.shape[1:], F32)
        for n in range(2, 4):
            c_land[n] = jnp.zeros((8, LANES), F32)

    @pl.when(is_top)
    def _():
        for copy in strip_straight:
            copy.wait_recv()
        for away, copy, _ in strip_mirrored:
            @pl.when(away)
            def _():
                copy.wait_recv()
        fold_strip(n_lon, lon_cells, stride, b, q_src, q_land, fp_v, fold_v)

    for copy in along:
        copy.wait_recv()

    for side, row in ((0, 0), (1, rows - PASSES)):
        for g in range(4):
            k = jnp.broadcast_to(kd_land[side, g : g + 1, :], (8, lat_cells))
            d = jnp.broadcast_to(kd_land[side, 4 + g : 5 + g, :], (8, lat_cells))
            w = jnp.where(d > wide_level.astype(F32), k, 0.0)
            kw[row + g] = w
            x = jnp.concatenate([x_land[side, 0, g], x_land[side, 1, g]], axis=0)
            y0[row + g] = x * w

    beyond = [spot < 4, jnp.logical_and(spot >= 8, spot < 12)]

    def edge_pieces(which, side):
        ref, edge = places[which]
        pieces = []
        for m in range(stride):
            packed = p_land[side, parts * which + m // 4]
            moved = roll(packed, (0 if side == 0 else 8) - 4 * (m % 4))
            pieces.append(jnp.where(beyond[side], moved, edge[1 - side, m]))
        for end, start in ((0, 0), (1, rows - PASSES)):
            corner = c_land[2 * side + end]
            for r in range(4):
                m, g = (start + r) % stride, (start + r) // stride
                at = 4 * (r + 4 * which)
                ghost = roll(corner, (0 if side == 0 else 8) + SLOT * g - at)
                own = jnp.where(inside[1 - side], outer(ref, 1 - side, start + r), 0.0)
                both = jnp.where(beyond[side], ghost, own)
                pieces[m] = jnp.where(lane // SLOT == g, both, pieces[m])
        return pieces

    def edge_sums(pieces):
        sums = []
        for m in range(stride):
            e = pieces[m + 1] if m < stride - 1 else roll(pieces[0], -SLOT)
            w = pieces[m - 1] if m else roll(pieces[stride - 1], SLOT)
            sums.append((roll(pieces[m], -1) + roll(pieces[m], 1)) + (e + w))
        return sums

    def finish(fold):
        def over_fold(step, pieces, side):
            if side == 0 or not fold:
                return pieces
            return [jnp.where(spot == 8, fold_v[step, m], pieces[m]) for m in range(stride)]

        edges, edge_c, edge_q = [], [], []
        for side in range(2):
            weights = over_fold(PASSES, edge_pieces(1, side), side)
            edge_c.append([1.0 - w * total for w, total in zip(weights, edge_sums(weights))])
            edge_q.append([w * w for w in weights])
            edges.append(edge_pieces(0, side))
        for n in range(PASSES):
            coefficients(1 + n)
            coefficients(rows - 2 - n)
        for step in range(PASSES):
            for side in range(2):
                pieces = over_fold(step, edges[side], side)
                edges[side] = [
                    c * y + q * total
                    for c, y, q, total in zip(edge_c[side], pieces, edge_q[side], edge_sums(pieces))
                ]
            for n in range(PASSES):
                advance(step, 1 + step + n)
                advance(step, rows - 2 - step - n)
        for side in range(2):
            for m in range(stride):
                edge_out[side, m] = edges[side][m]

    pl.when(has_n)(functools.partial(finish, False))
    pl.when(is_top)(functools.partial(finish, True))

    for copy in along:
        copy.wait_send()

    @pl.when(has_n)
    def _():
        for copy in up:
            copy.wait_send()

    @pl.when(has_s)
    def _():
        for copy in down:
            copy.wait_send()

    @pl.when(is_top)
    def _():
        for copy in strip_straight:
            copy.wait_send()
        for away, copy, _ in strip_mirrored:
            @pl.when(away)
            def _():
                copy.wait_send()


def balance_kernel(
    y_ref, edge_ref, inverse_ref, column_ref, elev_ref, ratio_ref,
    state_hbm, height_hbm, state_v, whole_v, height_v, sem,
):
    lon_cells, _, lat_cells = y_ref.shape
    stride = edge_ref.shape[1]
    tiles = lat_cells // LANES
    lane, sub = iotas()
    sigma = column_ref[0]
    expand = [jnp.broadcast_to(column_ref[1, s : s + 1, :], (8, LANES)) for s in range(8)]
    copies = []

    def send(src, dst):
        copies.append(pltpu.make_async_copy(src, dst, sem.at[len(copies)]))
        copies[-1].start()

    def balance(i):
        m, g = (i + PASSES) % stride, (i + PASSES) // stride
        for t in range(tiles):
            at = slice(LANES * t, LANES * (t + 1))
            y = y_ref[i, :, at]
            if t == 0:
                y = jnp.where(lane < 4, roll(edge_ref[0, m], -SLOT * g - 4), y)
            if t == tiles - 1:
                y = jnp.where(lane >= LANES - 4, roll(edge_ref[1, m], LANES - 8 - SLOT * g), y)
            scaled = y * (sigma * jnp.broadcast_to(inverse_ref[i : i + 1, at], (8, LANES)))
            ratio = jnp.broadcast_to(ratio_ref[i : i + 1, at], (8, LANES))
            state = scaled + jnp.where(sub >= 4, ratio * pltpu.roll(scaled, 4, 0), 0.0)
            state_v[0, i, :, at] = state[0:4]
            state_v[1, i, :, at] = state[4:8]
            whole_v[t, 8 * i : 8 * i + 8, :] = state

    done = 0
    for start in range(0, lon_cells, 8):
        count = min(8, lon_cells - start)
        for i in range(start, start + count):
            balance(i)
        for t in range(tiles):
            at = slice(LANES * t, LANES * (t + 1))
            height = elev_ref[start : start + count, at]
            for s in range(8):
                height = height + expand[s][0:count] * whole_v[t, pl.ds(8 * start + s, count, stride=8), :]
            height_v[start : start + count, at] = height
        if start + count - done >= 24 or start + count == lon_cells:
            part = pl.ds(done, start + count - done)
            send(state_v.at[:, part], state_hbm.at[:, part])
            done = start + count
    send(height_v, height_hbm)
    for copy in copies:
        copy.wait()


def local(
    n_lon, n_lat,
    control_fields,
    unexplained_elevation,
    diffusivity,
    depth_levels,
    fold_partner,
    prior_sigmas,
    haline_thermal_ratio,
    expansion_coefficients,
):
    levels, lon_cells, lat_cells = control_fields.shape[1:]
    fields = jnp.transpose(control_fields, (0, 2, 1, 3))
    stacked = 2 * levels
    rows = lon_cells + 2 * PASSES
    stride = -(-rows // GROUPS)
    parts = -(-stride // 4)
    vmem = pl.BlockSpec(memory_space=pltpu.VMEM)
    hbm = pl.BlockSpec(memory_space=pltpu.HBM)

    def shape(*dims):
        return jax.ShapeDtypeStruct(dims, F32)

    def tile(*dims):
        return pltpu.VMEM((*dims, 8, LANES), F32)

    def in_hbm(*arrays):
        return [pltpu.with_memory_space_constraint(array, pltpu.HBM) for array in arrays]

    passed = pl.pallas_call(
        functools.partial(diffuse_kernel, n_lon, n_lat),
        name="diffuse",
        out_shape=(
            shape(lon_cells, stacked, lat_cells),
            shape(2, stride, 8, LANES),
            shape(lon_cells, lat_cells),
            shape(2, 8, LANES),
        ),
        in_specs=[hbm] * 6,
        out_specs=(vmem,) * 4,
        scratch_shapes=[
            pltpu.VMEM(fields.shape, F32),
            pltpu.VMEM((lon_cells, lat_cells), F32),
            pltpu.VMEM((lon_cells, lat_cells), jnp.int32),
            pltpu.SMEM(fold_partner.shape, jnp.int32),
            pltpu.SMEM(prior_sigmas.shape, F32),
            pltpu.SMEM(expansion_coefficients.shape, F32),
            pltpu.VMEM((10, 8, LANES), jnp.int32),
            *[pltpu.VMEM((rows, 8, lat_cells), F32) for _ in range(7)],
            tile(2, stride),
            tile(2, stride),
            tile(PASSES + 1, stride),
            pltpu.VMEM((2, 8, lat_cells), F32),
            pltpu.VMEM((2, 2, 4, levels, lat_cells), F32),
            pltpu.VMEM((2, 8, lat_cells), F32),
            tile(2, 2 * parts + 2),
            tile(2, 2 * parts),
            tile(4),
            tile(6),
            tile(10, 6),
            pltpu.SemaphoreType.DMA((9,)),
            pltpu.SemaphoreType.DMA((20,)),
            pltpu.SemaphoreType.DMA((20,)),
        ],
        compiler_params=pltpu.CompilerParams(
            collective_id=0, has_side_effects=True, vmem_limit_bytes=40 * 1024 * 1024
        ),
    )(*in_hbm(fields, diffusivity, depth_levels, fold_partner, prior_sigmas, expansion_coefficients))
    state, height = pl.pallas_call(
        balance_kernel,
        name="balance",
        out_shape=(shape(*fields.shape), shape(lon_cells, lat_cells)),
        in_specs=[vmem] * 6,
        out_specs=(hbm, hbm),
        scratch_shapes=[
            pltpu.VMEM(fields.shape, F32),
            pltpu.VMEM((lat_cells // LANES, 8 * lon_cells, LANES), F32),
            pltpu.VMEM((lon_cells, lat_cells), F32),
            pltpu.SemaphoreType.DMA((8,)),
        ],
        compiler_params=pltpu.CompilerParams(vmem_limit_bytes=40 * 1024 * 1024),
    )(*passed, unexplained_elevation, haline_thermal_ratio)
    return jnp.transpose(state, (0, 2, 1, 3)), height


def solution(mesh):
    return jax.shard_map(
        functools.partial(local, mesh.shape["lon"], mesh.shape["lat"]),
        mesh=mesh,
        in_specs=(
            P(None, None, "lon", "lat"),
            P("lon", "lat"),
            P("lon", "lat"),
            P("lon", "lat"),
            P(),
            P(),
            P("lon", "lat"),
            P(),
        ),
        out_specs=(P(None, None, "lon", "lat"), P("lon", "lat")),
        check_vma=False,
    )
```

```python
import functools

import jax
import jax.numpy as jnp
from jax import lax
from jax.experimental import pallas as pl
from jax.experimental.pallas import tpu as pltpu
from jax.sharding import PartitionSpec as P

PASSES = 4
LANES = 128
SLOT = 16
GROUPS = LANES // SLOT
STRAIGHT_ROWS = (1, 2, 3, 2, 1)
MIRROR_ROWS = (2, 3, 4, 3, 2)
MESH = pl.DeviceIdType.MESH
F32 = jnp.float32


def strip_pieces(rows):
    return rows + (rows + 1) // 2


def iotas():
    shape = (8, LANES)
    return lax.broadcasted_iota(jnp.int32, shape, 1), lax.broadcasted_iota(jnp.int32, shape, 0)


def take(values, index):
    return jnp.take_along_axis(values, index, axis=1, mode="promise_in_bounds")


def roll(values, shift):
    shift = shift % LANES
    return pltpu.roll(values, shift, 1) if shift else values


def make_strip(stride, p_src, q_src):
    lane, sub = iotas()
    row_at = lane + PASSES
    m, g = row_at % stride, row_at // stride

    def row(r, parts):
        index = jnp.minimum(SLOT * g + 4 * (m % 4) + (PASSES - 1 - r), LANES - 1)
        result = take(parts[0], index)
        for n in range(1, len(parts)):
            result = jnp.where(m // 4 == n, take(parts[n], index), result)
        return result

    count = -(-stride // 4)
    fields = [p_src[0, n] for n in range(count)]
    weights = [p_src[0, count + n] for n in range(count)]
    for t in range(2):
        q_src[3 * t] = jnp.where(sub < 4, row(2 * t, weights), row(2 * t + 1, weights))
        for h in range(2):
            q_src[3 * t + 1 + h] = row(2 * t + h, fields)


def fold_blocks(n_lon, b):
    return {
        (kind, o): lax.rem((b if kind == "S" else -b) + o + 2 * n_lon, n_lon) for kind in "SM" for o in range(-2, 3)
    }


def fold_index(n_lon, lon_cells, b, fp_s, fp_v):
    lane, _ = iotas()
    blocks = list(fold_blocks(n_lon, b).values())

    def collect(l, rows):
        return tuple(
            jnp.where(lane == l, fp_s[block * lon_cells + l] - lax.rem(n_lon - block, n_lon) * lon_cells, row)
            for block, row in zip(blocks, rows)
        )

    nothing = jnp.zeros((8, LANES), jnp.int32)
    for n, row in enumerate(lax.fori_loop(0, lon_cells, collect, (nothing,) * len(blocks), unroll=4)):
        fp_v[n] = row


def fold_strip(n_lon, lon_cells, stride, b, q_src, q_land, fp_v, fold_v):
    lane, sub = iotas()
    index = {where: fp_v[n] for n, where in enumerate(fold_blocks(n_lon, b))}
    kinds = {"S": STRAIGHT_ROWS, "M": MIRROR_ROWS}
    y, kw = {}, {}
    for kind, rows in kinds.items():
        for o in range(-2, 3):
            slot = o + 2 + (0 if kind == "S" else 5)
            piece = (lambda i: q_src[i]) if slot == 2 else (lambda i, slot=slot: q_land[slot, i])
            for r in range(rows[o + 2]):
                t, h = r // 2, r % 2
                pair = piece(3 * t)
                turned = pltpu.roll(pair, 4, 0)
                kw[kind, o, r] = jnp.where((sub < 4) if h == 0 else (sub >= 4), pair, turned)
                y[kind, o, r] = piece(3 * t + 1 + h)

    other = {"S": "M", "M": "S"}

    def sides(table, kind, o, r):
        here = table[kind, o, r]
        from_east = table.get((kind, o + 1, r), here)
        from_west = table.get((kind, o - 1, r), here)
        return jnp.where(lane == lon_cells - 1, roll(from_east, lon_cells - 1), roll(here, -1)) + jnp.where(
            lane == 0, roll(from_west, 1 - lon_cells), roll(here, 1)
        )

    def above(table, kind, o, r):
        if r:
            return table[kind, o, r - 1]
        return take(table[other[kind], -o, 0], index[kind, o])

    def around(table, kind, o, r):
        return sides(table, kind, o, r) + above(table, kind, o, r) + table[kind, o, r + 1]

    slots = [jnp.minimum(m + stride * (lane // SLOT), LANES - 1) for m in range(stride)]

    def keep(n, table):
        own = take(table["M", 0, 0], index["S", 0])
        right = take(table["M", -1, 0], index["S", 1])
        left = take(table["M", 1, 0], index["S", -1])
        result = jnp.where(
            lane < 4, roll(left, 4 - lon_cells), jnp.where(lane < 4 + lon_cells, roll(own, 4), roll(right, 4 + lon_cells))
        )
        result = jnp.where(lane < 8 + lon_cells, result, 0.0)
        for m in range(stride):
            fold_v[n, m] = take(result, slots[m])

    keep(PASSES, kw)
    keep(0, y)
    coefficients = {}
    for step in range(1, PASSES):
        renewed = {}
        for kind, rows in kinds.items():
            for o in range(-2, 3):
                for r in range(rows[o + 2] - step):
                    if (kind, o, r) not in coefficients:
                        k0 = kw[kind, o, r]
                        coefficients[kind, o, r] = 1.0 - k0 * around(kw, kind, o, r), k0 * k0
                    c, q = coefficients[kind, o, r]
                    renewed[kind, o, r] = c * y[kind, o, r] + q * around(y, kind, o, r)
        y.update(renewed)
        keep(step, y)


def diffuse_kernel(
    n_lon, n_lat,
    x_hbm, k_hbm, d_hbm, fp_hbm, sigma_hbm, expand_hbm,
    y_out, edge_out, inverse_out, column_out,
    x_v, k_v, d_v, fp_s, sigma_s, expand_s, fp_v,
    y0, y1, y2, y3, kw, cc, qq, edge_y, edge_kw, fold_v,
    kd_src, x_land, kd_land, p_src, p_land, c_land, q_src, q_land,
    local_sem, send_sem, recv_sem, ready_sem,
):
    lon_cells, lat_cells = k_hbm.shape
    rows = lon_cells + 2 * PASSES
    stride = edge_y.shape[1]
    parts = -(-stride // 4)
    tiles = lat_cells // LANES
    b = lax.axis_index("lon")
    a = lax.axis_index("lat")
    has_n = a < n_lat - 1
    has_s = a > 0
    is_top = a == n_lat - 1
    first_lon = b == 0
    east = lax.rem(b + 1, n_lon)
    west = lax.rem(b + n_lon - 1, n_lon)
    north = lax.rem(a + 1, n_lat)
    south = lax.rem(a + n_lat - 1, n_lat)
    lane, sub = iotas()
    spot = lane % SLOT

    straight = [
        (slot, STRAIGHT_ROWS[slot], lax.rem(b - (slot - 2) + n_lon, n_lon)) for slot in (0, 1, 3, 4)
    ]
    mirrored = [
        (5 + slot, MIRROR_ROWS[slot], lax.rem((slot - 2) - b + 2 * n_lon, n_lon)) for slot in range(5)
    ]

    barrier = pltpu.get_barrier_semaphore()

    def hail(lon, lat):
        pl.semaphore_signal(barrier, inc=1, device_id={"lon": lon, "lat": lat}, device_id_type=MESH)

    hail(west, a)
    hail(east, a)

    @pl.when(has_n)
    def _():
        for lon in (b, east, west):
            hail(lon, north)

    def at_seam(lon):
        return jnp.logical_or(first_lon, lon == 0)

    for lon in (b, east, west):
        @pl.when(jnp.logical_and(has_s, at_seam(lon)))
        def _(lon=lon):
            hail(lon, south)

    seam_count = sum(jnp.where(at_seam(lon), 1, 0) for lon in (b, east, west))

    @pl.when(is_top)
    def _():
        for _, _, target in straight:
            hail(target, a)
        for _, _, target in mirrored:
            @pl.when(target != b)
            def _():
                hail(target, a)

    expected = 2 + jnp.where(has_s, 3, 0) + jnp.where(has_n, seam_count, 0) + jnp.where(is_top, 4, 0)
    for _, _, target in mirrored:
        expected = expected + jnp.where(jnp.logical_and(is_top, target != b), 1, 0)

    def enter():
        pl.semaphore_wait(barrier, expected)

        for lon in (b, east, west):
            @pl.when(jnp.logical_and(has_s, jnp.logical_not(at_seam(lon))))
            def _(lon=lon):
                pl.semaphore_signal(
                    ready_sem, inc=1, device_id={"lon": lon, "lat": south}, device_id_type=MESH
                )

    chunk = 17
    load_k = pltpu.make_async_copy(k_hbm, k_v, local_sem.at[0])
    load_d = pltpu.make_async_copy(d_hbm, d_v, local_sem.at[1])
    small = [
        pltpu.make_async_copy(fp_hbm, fp_s, local_sem.at[2]),
        pltpu.make_async_copy(sigma_hbm, sigma_s, local_sem.at[3]),
        pltpu.make_async_copy(expand_hbm, expand_s, local_sem.at[4]),
    ]
    loads = [
        pltpu.make_async_copy(
            x_hbm.at[:, pl.ds(chunk * n, chunk)], x_v.at[:, pl.ds(chunk * n, chunk)], local_sem.at[5 + n]
        )
        for n in range(lon_cells // chunk)
    ]
    for copy in [load_k, load_d, loads[0], loads[-1], *loads[1:-1], *small]:
        copy.start()

    def remote(src, dst, index, lon, lat):
        return pltpu.make_async_remote_copy(
            src_ref=src, dst_ref=dst, send_sem=send_sem.at[index], recv_sem=recv_sem.at[index],
            device_id={"lon": lon, "lat": lat}, device_id_type=MESH,
        )

    along = [
        remote(x_hbm.at[:, pl.ds(lon_cells - 4, 4)], x_land.at[0], 0, east, a),
        remote(x_hbm.at[:, pl.ds(0, 4)], x_land.at[1], 1, west, a),
        remote(kd_src.at[0], kd_land.at[0], 2, east, a),
        remote(kd_src.at[1], kd_land.at[1], 3, west, a),
    ]
    whole = pl.ds(0, 2 * parts)
    up = [
        remote(p_src.at[0, whole], p_land.at[0], 4, b, north),
        remote(p_src.at[0, 2 * parts], c_land.at[0], 6, east, north),
        remote(p_src.at[0, 2 * parts + 1], c_land.at[1], 7, west, north),
    ]
    down = [
        remote(p_src.at[1, whole], p_land.at[1], 5, b, south),
        remote(p_src.at[1, 2 * parts], c_land.at[2], 8, east, south),
        remote(p_src.at[1, 2 * parts + 1], c_land.at[3], 9, west, south),
    ]

    def strip(slot, count, target):
        part = pl.ds(0, strip_pieces(count))
        return remote(q_src.at[part], q_land.at[slot, part], 10 + slot, target, a)

    strip_straight = [strip(*which) for which in straight]
    strip_mirrored = [(which[2] != b, strip(*which), which[0]) for which in mirrored]

    def send_fields():
        for copy in along[:2]:
            copy.start()

    def send_weights():
        for copy in along[2:]:
            copy.start()

    def send_down():
        @pl.when(has_s)
        def _():
            for copy in down[1:]:
                copy.start()

    def send_up():
        @pl.when(has_n)
        def _():
            @pl.when(jnp.logical_not(first_lon))
            def _():
                pl.semaphore_wait(ready_sem, 3 - seam_count)

            for copy in up:
                copy.start()

    def send_edges():
        @pl.when(has_s)
        def _():
            down[0].start()

        send_up()

    at_once = jnp.logical_not(jnp.logical_or(first_lon, jnp.logical_and(is_top, b < n_lon - 1)))
    last = jnp.logical_and(first_lon, jnp.logical_not(is_top))

    @pl.when(at_once)
    def _():
        enter()
        send_fields()

    load_k.wait()
    load_d.wait()
    kd_src[0, 0:4] = k_v[lon_cells - 4 : lon_cells, :]
    kd_src[0, 4:8] = d_v[lon_cells - 4 : lon_cells, :].astype(F32)
    kd_src[1, 0:4] = k_v[0:4, :]
    kd_src[1, 4:8] = d_v[0:4, :].astype(F32)

    pl.when(at_once)(send_weights)

    loads[0].wait()
    loads[-1].wait()
    level = sub % 4
    wide_level = lax.broadcasted_iota(jnp.int32, (8, lat_cells), 0) % 4

    for side in range(2):
        tile = slice(lat_cells - LANES, lat_cells) if side == 0 else slice(0, LANES)
        for end, start in ((0, lon_cells - 4), (1, 0)):
            corner = jnp.zeros((8, LANES), F32)
            for r in range(4):
                i = start + r
                k = jnp.broadcast_to(k_v[i : i + 1, tile], (8, LANES))
                d = jnp.broadcast_to(d_v[i : i + 1, tile], (8, LANES))
                weight = jnp.where(d > level, k, 0.0)
                field = jnp.concatenate([x_v[0, i, :, tile], x_v[1, i, :, tile]], axis=0) * weight
                for at, value in ((4 * r, field), (4 * (r + 4), weight)):
                    moved = roll(value, at + (4 if side == 0 else 0))
                    corner = jnp.where(jnp.logical_and(lane >= at, lane < at + 4), moved, corner)
            p_src[side, 2 * parts + end] = corner

    pl.when(at_once)(send_down)

    def own_weights(i, carry):
        k = jnp.broadcast_to(k_v[pl.ds(i, 1), :], (8, lat_cells))
        d = jnp.broadcast_to(d_v[pl.ds(i, 1), :], (8, lat_cells))
        kw[i + PASSES] = jnp.where(d > wide_level, k, 0.0)
        return carry

    lax.fori_loop(0, lon_cells, own_weights, 0, unroll=17)
    for copy in loads[1:-1]:
        copy.wait()

    def own_fields(i, carry):
        x = jnp.concatenate([x_v[0, i], x_v[1, i]], axis=0)
        y0[i + PASSES] = x * kw[i + PASSES]
        return carry

    lax.fori_loop(0, lon_cells, own_fields, 0, unroll=17)

    def outer(ref, side, row):
        g = row // stride
        if side == 0:
            return roll(ref[row, :, lat_cells - LANES : lat_cells], SLOT * g + 8)
        return roll(ref[row, :, 0:LANES], SLOT * g + 4)

    inside = [spot < 8, jnp.logical_and(spot >= 4, spot < 12)]
    places = ((y0, edge_y), (kw, edge_kw))
    for side in range(2):
        for which, (ref, edge) in enumerate(places):
            pieces = []
            for m in range(stride):
                piece = jnp.zeros((8, LANES), F32)
                for g in range(GROUPS):
                    row = m + stride * g
                    if PASSES <= row < rows - PASSES:
                        piece = jnp.where(lane >= SLOT * g, outer(ref, side, row), piece)
                    elif row >= rows - PASSES:
                        piece = jnp.where(lane >= SLOT * g, 0.0, piece)
                piece = jnp.where(inside[side], piece, 0.0)
                edge[side, m] = piece
                pieces.append(piece)
            for n in range(parts):
                packed = jnp.zeros((8, LANES), F32)
                for t in range(4):
                    if 4 * n + t < stride:
                        packed = jnp.where(spot // 4 == t, roll(pieces[4 * n + t], 4 * t - 4), packed)
                p_src[side, parts * which + n] = packed

    pl.when(jnp.logical_and(at_once, jnp.logical_not(is_top)))(send_edges)

    @pl.when(is_top)
    def _():
        make_strip(stride, p_src, q_src)
        @pl.when(jnp.logical_not(at_once))
        def _():
            enter()

        for copy in strip_straight:
            copy.start()
        for away, copy, slot in strip_mirrored:
            @pl.when(away)
            def _():
                copy.start()

            @pl.when(jnp.logical_not(away))
            def _():
                q_land[slot] = q_src[...]
        send_edges()

        @pl.when(jnp.logical_not(at_once))
        def _():
            send_down()
            send_fields()
            send_weights()

    for copy in small:
        copy.wait()

    @pl.when(is_top)
    def _():
        fold_index(n_lon, lon_cells, b, fp_s, fp_v)

    @pl.when(jnp.logical_and(last, a >= n_lat // 2))
    def _():
        enter()

        @pl.when(has_s)
        def _():
            down[0].start()

        send_down()
        send_fields()
        send_weights()
        send_up()

    for n, ref in enumerate((sigma_s, expand_s)):
        column = jnp.zeros((8, LANES), F32)
        for c in range(2):
            for level in range(4):
                column = jnp.where(sub == 4 * c + level, ref[c, level], column)
        column_out[n] = column
    inverse_out[...] = 1.0 / k_v[...]

    def lattice(ref, row):
        here = [ref[row, :, LANES * t : LANES * (t + 1)] for t in range(tiles)]
        up_one = [roll(v, -1) for v in here]
        down_one = [roll(v, 1) for v in here]
        sums = []
        for t in range(tiles):
            n = jnp.where(lane == LANES - 1, up_one[(t + 1) % tiles], up_one[t])
            s = jnp.where(lane == 0, down_one[t - 1], down_one[t])
            at = slice(LANES * t, LANES * (t + 1))
            sums.append((n + s) + (ref[row + 1, :, at] + ref[row - 1, :, at]))
        return here, sums

    def coefficients(row):
        here, sums = lattice(kw, row)
        for t in range(tiles):
            cc[row, :, LANES * t : LANES * (t + 1)] = 1.0 - here[t] * sums[t]
            qq[row, :, LANES * t : LANES * (t + 1)] = here[t] * here[t]

    states = [y0, y1, y2, y3]

    def advance(step, row):
        here, sums = lattice(states[step], row)
        for t in range(tiles):
            at = slice(LANES * t, LANES * (t + 1))
            new = cc[row, :, at] * here[t] + qq[row, :, at] * sums[t]
            if step < PASSES - 1:
                states[step + 1][row, :, at] = new
            else:
                y_out[row - PASSES, :, at] = new

    def over_rows(first, last, body, unroll):
        def one(row, carry):
            body(row)
            return carry

        lax.fori_loop(first, last, one, 0, unroll=unroll)

    over_rows(PASSES + 1, rows - PASSES - 1, coefficients, 33)
    for step in range(PASSES):
        over_rows(PASSES + 1 + step, rows - PASSES - 1 - step, functools.partial(advance, step), 33 - step)

    @pl.when(jnp.logical_and(last, a < n_lat // 2))
    def _():
        enter()

        @pl.when(has_s)
        def _():
            down[0].start()

        send_down()
        send_fields()
        send_weights()
        send_up()

    @pl.when(has_s)
    def _():
        for copy in up:
            copy.wait_recv()

    @pl.when(jnp.logical_not(has_s))
    def _():
        p_land[0] = jnp.zeros(p_land.shape[1:], F32)
        for n in range(2):
            c_land[n] = jnp.zeros((8, LANES), F32)

    @pl.when(has_n)
    def _():
        for copy in down:
            copy.wait_recv()

    @pl.when(is_top)
    def _():
        p_land[1] = jnp.zeros(p_land.shape[1:], F32)
        for n in range(2, 4):
            c_land[n] = jnp.zeros((8, LANES), F32)

    @pl.when(is_top)
    def _():
        for copy in strip_straight:
            copy.wait_recv()
        for away, copy, _ in strip_mirrored:
            @pl.when(away)
            def _():
                copy.wait_recv()
        fold_strip(n_lon, lon_cells, stride, b, q_src, q_land, fp_v, fold_v)

    for copy in along:
        copy.wait_recv()

    for side, row in ((0, 0), (1, rows - PASSES)):
        for g in range(4):
            k = jnp.broadcast_to(kd_land[side, g : g + 1, :], (8, lat_cells))
            d = jnp.broadcast_to(kd_land[side, 4 + g : 5 + g, :], (8, lat_cells))
            w = jnp.where(d > wide_level.astype(F32), k, 0.0)
            kw[row + g] = w
            x = jnp.concatenate([x_land[side, 0, g], x_land[side, 1, g]], axis=0)
            y0[row + g] = x * w

    beyond = [spot < 4, jnp.logical_and(spot >= 8, spot < 12)]

    def edge_pieces(which, side):
        ref, edge = places[which]
        pieces = []
        for m in range(stride):
            packed = p_land[side, parts * which + m // 4]
            moved = roll(packed, (0 if side == 0 else 8) - 4 * (m % 4))
            pieces.append(jnp.where(beyond[side], moved, edge[1 - side, m]))
        for end, start in ((0, 0), (1, rows - PASSES)):
            corner = c_land[2 * side + end]
            for r in range(4):
                m, g = (start + r) % stride, (start + r) // stride
                at = 4 * (r + 4 * which)
                ghost = roll(corner, (0 if side == 0 else 8) + SLOT * g - at)
                own = jnp.where(inside[1 - side], outer(ref, 1 - side, start + r), 0.0)
                both = jnp.where(beyond[side], ghost, own)
                pieces[m] = jnp.where(lane // SLOT == g, both, pieces[m])
        return pieces

    def edge_sums(pieces):
        sums = []
        for m in range(stride):
            e = pieces[m + 1] if m < stride - 1 else roll(pieces[0], -SLOT)
            w = pieces[m - 1] if m else roll(pieces[stride - 1], SLOT)
            sums.append((roll(pieces[m], -1) + roll(pieces[m], 1)) + (e + w))
        return sums

    def finish(fold):
        def over_fold(step, pieces, side):
            if side == 0 or not fold:
                return pieces
            return [jnp.where(spot == 8, fold_v[step, m], pieces[m]) for m in range(stride)]

        edges, edge_c, edge_q = [], [], []
        for side in range(2):
            weights = over_fold(PASSES, edge_pieces(1, side), side)
            edge_c.append([1.0 - w * total for w, total in zip(weights, edge_sums(weights))])
            edge_q.append([w * w for w in weights])
            edges.append(edge_pieces(0, side))
        for n in range(PASSES):
            coefficients(1 + n)
            coefficients(rows - 2 - n)
        for step in range(PASSES):
            for side in range(2):
                pieces = over_fold(step, edges[side], side)
                edges[side] = [
                    c * y + q * total
                    for c, y, q, total in zip(edge_c[side], pieces, edge_q[side], edge_sums(pieces))
                ]
            for n in range(PASSES):
                advance(step, 1 + step + n)
                advance(step, rows - 2 - step - n)
        for side in range(2):
            for m in range(stride):
                edge_out[side, m] = edges[side][m]

    pl.when(has_n)(functools.partial(finish, False))
    pl.when(is_top)(functools.partial(finish, True))

    for copy in along:
        copy.wait_send()

    @pl.when(has_n)
    def _():
        for copy in up:
            copy.wait_send()

    @pl.when(has_s)
    def _():
        for copy in down:
            copy.wait_send()

    @pl.when(is_top)
    def _():
        for copy in strip_straight:
            copy.wait_send()
        for away, copy, _ in strip_mirrored:
            @pl.when(away)
            def _():
                copy.wait_send()


def balance_kernel(
    y_ref, edge_ref, inverse_ref, column_ref, elev_ref, ratio_ref,
    state_hbm, height_hbm, state_v, whole_v, height_v, sem,
):
    lon_cells, _, lat_cells = y_ref.shape
    stride = edge_ref.shape[1]
    tiles = lat_cells // LANES
    lane, sub = iotas()
    sigma = column_ref[0]
    expand = [jnp.broadcast_to(column_ref[1, s : s + 1, :], (8, LANES)) for s in range(8)]
    copies = []

    def send(src, dst):
        copies.append(pltpu.make_async_copy(src, dst, sem.at[len(copies)]))
        copies[-1].start()

    def balance(i):
        m, g = (i + PASSES) % stride, (i + PASSES) // stride
        for t in range(tiles):
            at = slice(LANES * t, LANES * (t + 1))
            y = y_ref[i, :, at]
            if t == 0:
                y = jnp.where(lane < 4, roll(edge_ref[0, m], -SLOT * g - 4), y)
            if t == tiles - 1:
                y = jnp.where(lane >= LANES - 4, roll(edge_ref[1, m], LANES - 8 - SLOT * g), y)
            scaled = y * (sigma * jnp.broadcast_to(inverse_ref[i : i + 1, at], (8, LANES)))
            ratio = jnp.broadcast_to(ratio_ref[i : i + 1, at], (8, LANES))
            state = scaled + jnp.where(sub >= 4, ratio * pltpu.roll(scaled, 4, 0), 0.0)
            state_v[0, i, :, at] = state[0:4]
            state_v[1, i, :, at] = state[4:8]
            whole_v[t, 8 * i : 8 * i + 8, :] = state

    done = 0
    for start in range(0, lon_cells, 8):
        count = min(8, lon_cells - start)
        for i in range(start, start + count):
            balance(i)
        for t in range(tiles):
            at = slice(LANES * t, LANES * (t + 1))
            height = elev_ref[start : start + count, at]
            for s in range(8):
                height = height + expand[s][0:count] * whole_v[t, pl.ds(8 * start + s, count, stride=8), :]
            height_v[start : start + count, at] = height
        if start + count - done >= 24 or start + count == lon_cells:
            part = pl.ds(done, start + count - done)
            send(state_v.at[:, part], state_hbm.at[:, part])
            done = start + count
    send(height_v, height_hbm)
    for copy in copies:
        copy.wait()


def local(
    n_lon, n_lat,
    control_fields,
    unexplained_elevation,
    diffusivity,
    depth_levels,
    fold_partner,
    prior_sigmas,
    haline_thermal_ratio,
    expansion_coefficients,
):
    levels, lon_cells, lat_cells = control_fields.shape[1:]
    fields = jnp.transpose(control_fields, (0, 2, 1, 3))
    stacked = 2 * levels
    rows = lon_cells + 2 * PASSES
    stride = -(-rows // GROUPS)
    parts = -(-stride // 4)
    vmem = pl.BlockSpec(memory_space=pltpu.VMEM)
    hbm = pl.BlockSpec(memory_space=pltpu.HBM)

    def shape(*dims):
        return jax.ShapeDtypeStruct(dims, F32)

    def tile(*dims):
        return pltpu.VMEM((*dims, 8, LANES), F32)

    def in_hbm(*arrays):
        return [pltpu.with_memory_space_constraint(array, pltpu.HBM) for array in arrays]

    passed = pl.pallas_call(
        functools.partial(diffuse_kernel, n_lon, n_lat),
        name="diffuse",
        out_shape=(
            shape(lon_cells, stacked, lat_cells),
            shape(2, stride, 8, LANES),
            shape(lon_cells, lat_cells),
            shape(2, 8, LANES),
        ),
        in_specs=[hbm] * 6,
        out_specs=(vmem,) * 4,
        scratch_shapes=[
            pltpu.VMEM(fields.shape, F32),
            pltpu.VMEM((lon_cells, lat_cells), F32),
            pltpu.VMEM((lon_cells, lat_cells), jnp.int32),
            pltpu.SMEM(fold_partner.shape, jnp.int32),
            pltpu.SMEM(prior_sigmas.shape, F32),
            pltpu.SMEM(expansion_coefficients.shape, F32),
            pltpu.VMEM((10, 8, LANES), jnp.int32),
            *[pltpu.VMEM((rows, 8, lat_cells), F32) for _ in range(7)],
            tile(2, stride),
            tile(2, stride),
            tile(PASSES + 1, stride),
            pltpu.VMEM((2, 8, lat_cells), F32),
            pltpu.VMEM((2, 2, 4, levels, lat_cells), F32),
            pltpu.VMEM((2, 8, lat_cells), F32),
            tile(2, 2 * parts + 2),
            tile(2, 2 * parts),
            tile(4),
            tile(6),
            tile(10, 6),
            pltpu.SemaphoreType.DMA((9,)),
            pltpu.SemaphoreType.DMA((20,)),
            pltpu.SemaphoreType.DMA((20,)),
            pltpu.SemaphoreType.REGULAR,
        ],
        compiler_params=pltpu.CompilerParams(
            collective_id=0, has_side_effects=True, vmem_limit_bytes=40 * 1024 * 1024
        ),
    )(*in_hbm(fields, diffusivity, depth_levels, fold_partner, prior_sigmas, expansion_coefficients))
    state, height = pl.pallas_call(
        balance_kernel,
        name="balance",
        out_shape=(shape(*fields.shape), shape(lon_cells, lat_cells)),
        in_specs=[vmem] * 6,
        out_specs=(hbm, hbm),
        scratch_shapes=[
            pltpu.VMEM(fields.shape, F32),
            pltpu.VMEM((lat_cells // LANES, 8 * lon_cells, LANES), F32),
            pltpu.VMEM((lon_cells, lat_cells), F32),
            pltpu.SemaphoreType.DMA((8,)),
        ],
        compiler_params=pltpu.CompilerParams(vmem_limit_bytes=40 * 1024 * 1024),
    )(*passed, unexplained_elevation, haline_thermal_ratio)
    return jnp.transpose(state, (0, 2, 1, 3)), height


def solution(mesh):
    return jax.shard_map(
        functools.partial(local, mesh.shape["lon"], mesh.shape["lat"]),
        mesh=mesh,
        in_specs=(
            P(None, None, "lon", "lat"),
            P("lon", "lat"),
            P("lon", "lat"),
            P("lon", "lat"),
            P(),
            P(),
            P("lon", "lat"),
            P(),
        ),
        out_specs=(P(None, None, "lon", "lat"), P("lon", "lat")),
        check_vma=False,
    )
```

```python
import functools

import jax
import jax.numpy as jnp
from jax import lax
from jax.experimental import pallas as pl
from jax.experimental.pallas import tpu as pltpu
from jax.sharding import PartitionSpec as P

PASSES = 4
LANES = 128
SLOT = 16
GROUPS = LANES // SLOT
STRAIGHT_ROWS = (1, 2, 3, 2, 1)
MIRROR_ROWS = (2, 3, 4, 3, 2)
MESH = pl.DeviceIdType.MESH
F32 = jnp.float32


def strip_pieces(rows):
    return rows + (rows + 1) // 2


def iotas():
    shape = (8, LANES)
    return lax.broadcasted_iota(jnp.int32, shape, 1), lax.broadcasted_iota(jnp.int32, shape, 0)


def take(values, index):
    return jnp.take_along_axis(values, index, axis=1, mode="promise_in_bounds")


def roll(values, shift):
    shift = shift % LANES
    return pltpu.roll(values, shift, 1) if shift else values


def make_strip(stride, p_src, q_src):
    lane, sub = iotas()
    row_at = lane + PASSES
    m, g = row_at % stride, row_at // stride

    def row(r, parts):
        index = jnp.minimum(SLOT * g + 4 * (m % 4) + (PASSES - 1 - r), LANES - 1)
        result = take(parts[0], index)
        for n in range(1, len(parts)):
            result = jnp.where(m // 4 == n, take(parts[n], index), result)
        return result

    count = -(-stride // 4)
    fields = [p_src[0, n] for n in range(count)]
    weights = [p_src[0, count + n] for n in range(count)]
    for t in range(2):
        q_src[3 * t] = jnp.where(sub < 4, row(2 * t, weights), row(2 * t + 1, weights))
        for h in range(2):
            q_src[3 * t + 1 + h] = row(2 * t + h, fields)


def fold_blocks(n_lon, b):
    return {
        (kind, o): lax.rem((b if kind == "S" else -b) + o + 2 * n_lon, n_lon) for kind in "SM" for o in range(-2, 3)
    }


def fold_index(n_lon, lon_cells, b, fp_s, fp_v):
    lane, _ = iotas()
    blocks = list(fold_blocks(n_lon, b).values())

    def collect(l, rows):
        return tuple(
            jnp.where(lane == l, fp_s[block * lon_cells + l] - lax.rem(n_lon - block, n_lon) * lon_cells, row)
            for block, row in zip(blocks, rows)
        )

    nothing = jnp.zeros((8, LANES), jnp.int32)
    for n, row in enumerate(lax.fori_loop(0, lon_cells, collect, (nothing,) * len(blocks), unroll=4)):
        fp_v[n] = row


def fold_strip(n_lon, lon_cells, stride, b, q_src, q_land, fp_v, fold_v):
    lane, sub = iotas()
    index = {where: fp_v[n] for n, where in enumerate(fold_blocks(n_lon, b))}
    kinds = {"S": STRAIGHT_ROWS, "M": MIRROR_ROWS}
    y, kw = {}, {}
    for kind, rows in kinds.items():
        for o in range(-2, 3):
            slot = o + 2 + (0 if kind == "S" else 5)
            piece = (lambda i: q_src[i]) if slot == 2 else (lambda i, slot=slot: q_land[slot, i])
            for r in range(rows[o + 2]):
                t, h = r // 2, r % 2
                pair = piece(3 * t)
                turned = pltpu.roll(pair, 4, 0)
                kw[kind, o, r] = jnp.where((sub < 4) if h == 0 else (sub >= 4), pair, turned)
                y[kind, o, r] = piece(3 * t + 1 + h)

    other = {"S": "M", "M": "S"}

    def sides(table, kind, o, r):
        here = table[kind, o, r]
        from_east = table.get((kind, o + 1, r), here)
        from_west = table.get((kind, o - 1, r), here)
        return jnp.where(lane == lon_cells - 1, roll(from_east, lon_cells - 1), roll(here, -1)) + jnp.where(
            lane == 0, roll(from_west, 1 - lon_cells), roll(here, 1)
        )

    def above(table, kind, o, r):
        if r:
            return table[kind, o, r - 1]
        return take(table[other[kind], -o, 0], index[kind, o])

    def around(table, kind, o, r):
        return sides(table, kind, o, r) + above(table, kind, o, r) + table[kind, o, r + 1]

    slots = [jnp.minimum(m + stride * (lane // SLOT), LANES - 1) for m in range(stride)]

    def keep(n, table):
        own = take(table["M", 0, 0], index["S", 0])
        right = take(table["M", -1, 0], index["S", 1])
        left = take(table["M", 1, 0], index["S", -1])
        result = jnp.where(
            lane < 4, roll(left, 4 - lon_cells), jnp.where(lane < 4 + lon_cells, roll(own, 4), roll(right, 4 + lon_cells))
        )
        result = jnp.where(lane < 8 + lon_cells, result, 0.0)
        for m in range(stride):
            fold_v[n, m] = take(result, slots[m])

    keep(PASSES, kw)
    keep(0, y)
    coefficients = {}
    for step in range(1, PASSES):
        renewed = {}
        for kind, rows in kinds.items():
            for o in range(-2, 3):
                for r in range(rows[o + 2] - step):
                    if (kind, o, r) not in coefficients:
                        k0 = kw[kind, o, r]
                        coefficients[kind, o, r] = 1.0 - k0 * around(kw, kind, o, r), k0 * k0
                    c, q = coefficients[kind, o, r]
                    renewed[kind, o, r] = c * y[kind, o, r] + q * around(y, kind, o, r)
        y.update(renewed)
        keep(step, y)


def diffuse_kernel(
    n_lon, n_lat,
    x_hbm, k_hbm, d_hbm, fp_hbm, sigma_hbm, expand_hbm,
    y_out, edge_out, inverse_out, column_out,
    x_v, k_v, d_v, fp_s, sigma_s, expand_s, fp_v,
    y0, y1, y2, y3, kw, cc, qq, edge_y, edge_kw, fold_v,
    kd_src, x_land, kd_land, p_src, p_land, c_land, q_src, q_land,
    local_sem, send_sem, recv_sem, ready_sem,
):
    lon_cells, lat_cells = k_hbm.shape
    rows = lon_cells + 2 * PASSES
    stride = edge_y.shape[1]
    parts = -(-stride // 4)
    tiles = lat_cells // LANES
    b = lax.axis_index("lon")
    a = lax.axis_index("lat")
    has_n = a < n_lat - 1
    has_s = a > 0
    is_top = a == n_lat - 1
    first_lon = b == 0
    east = lax.rem(b + 1, n_lon)
    west = lax.rem(b + n_lon - 1, n_lon)
    north = lax.rem(a + 1, n_lat)
    south = lax.rem(a + n_lat - 1, n_lat)
    lane, sub = iotas()
    spot = lane % SLOT

    straight = [
        (slot, STRAIGHT_ROWS[slot], lax.rem(b - (slot - 2) + n_lon, n_lon)) for slot in (0, 1, 3, 4)
    ]
    mirrored = [
        (5 + slot, MIRROR_ROWS[slot], lax.rem((slot - 2) - b + 2 * n_lon, n_lon)) for slot in range(5)
    ]

    barrier = pltpu.get_barrier_semaphore()

    def hail(lon, lat):
        pl.semaphore_signal(barrier, inc=1, device_id={"lon": lon, "lat": lat}, device_id_type=MESH)

    hail(west, a)
    hail(east, a)

    @pl.when(has_n)
    def _():
        for lon in (b, east, west):
            hail(lon, north)

    def at_seam(lon):
        return jnp.logical_or(first_lon, lon == 0)

    for lon in (b, east, west):
        @pl.when(jnp.logical_and(has_s, at_seam(lon)))
        def _(lon=lon):
            hail(lon, south)

    seam_count = sum(jnp.where(at_seam(lon), 1, 0) for lon in (b, east, west))

    @pl.when(is_top)
    def _():
        for _, _, target in straight:
            hail(target, a)
        for _, _, target in mirrored:
            @pl.when(target != b)
            def _():
                hail(target, a)

    expected = 2 + jnp.where(has_s, 3, 0) + jnp.where(has_n, seam_count, 0) + jnp.where(is_top, 4, 0)
    for _, _, target in mirrored:
        expected = expected + jnp.where(jnp.logical_and(is_top, target != b), 1, 0)

    def enter():
        pl.semaphore_wait(barrier, expected)

        for lon in (b, east, west):
            @pl.when(jnp.logical_and(has_s, jnp.logical_not(at_seam(lon))))
            def _(lon=lon):
                pl.semaphore_signal(
                    ready_sem, inc=1, device_id={"lon": lon, "lat": south}, device_id_type=MESH
                )

    chunk = 17
    load_k = pltpu.make_async_copy(k_hbm, k_v, local_sem.at[0])
    load_d = pltpu.make_async_copy(d_hbm, d_v, local_sem.at[1])
    small = [
        pltpu.make_async_copy(fp_hbm, fp_s, local_sem.at[2]),
        pltpu.make_async_copy(sigma_hbm, sigma_s, local_sem.at[3]),
        pltpu.make_async_copy(expand_hbm, expand_s, local_sem.at[4]),
    ]
    loads = [
        pltpu.make_async_copy(
            x_hbm.at[:, pl.ds(chunk * n, chunk)], x_v.at[:, pl.ds(chunk * n, chunk)], local_sem.at[5 + n]
        )
        for n in range(lon_cells // chunk)
    ]
    for copy in [load_k, load_d, loads[-1], loads[0], *loads[1:-1], *small]:
        copy.start()

    def remote(src, dst, index, lon, lat):
        return pltpu.make_async_remote_copy(
            src_ref=src, dst_ref=dst, send_sem=send_sem.at[index], recv_sem=recv_sem.at[index],
            device_id={"lon": lon, "lat": lat}, device_id_type=MESH,
        )

    along = [
        remote(x_v.at[:, pl.ds(lon_cells - 4, 4)], x_land.at[0], 0, east, a),
        remote(x_v.at[:, pl.ds(0, 4)], x_land.at[1], 1, west, a),
        remote(kd_src.at[0], kd_land.at[0], 2, east, a),
        remote(kd_src.at[1], kd_land.at[1], 3, west, a),
    ]
    whole = pl.ds(0, 2 * parts)
    up = [
        remote(p_src.at[0, whole], p_land.at[0], 4, b, north),
        remote(p_src.at[0, 2 * parts], c_land.at[0], 6, east, north),
        remote(p_src.at[0, 2 * parts + 1], c_land.at[1], 7, west, north),
    ]
    down = [
        remote(p_src.at[1, whole], p_land.at[1], 5, b, south),
        remote(p_src.at[1, 2 * parts], c_land.at[2], 8, east, south),
        remote(p_src.at[1, 2 * parts + 1], c_land.at[3], 9, west, south),
    ]

    def strip(slot, count, target):
        part = pl.ds(0, strip_pieces(count))
        return remote(q_src.at[part], q_land.at[slot, part], 10 + slot, target, a)

    strip_straight = [strip(*which) for which in straight]
    strip_mirrored = [(which[2] != b, strip(*which), which[0]) for which in mirrored]

    def send_fields():
        for copy in along[:2]:
            copy.start()

    def send_weights():
        for copy in along[2:]:
            copy.start()

    def send_down():
        @pl.when(has_s)
        def _():
            for copy in down[1:]:
                copy.start()

    def send_up():
        @pl.when(has_n)
        def _():
            @pl.when(jnp.logical_not(first_lon))
            def _():
                pl.semaphore_wait(ready_sem, 3 - seam_count)

            for copy in up:
                copy.start()

    def send_edges():
        @pl.when(has_s)
        def _():
            down[0].start()

        send_up()

    at_once = jnp.logical_not(jnp.logical_or(first_lon, jnp.logical_and(is_top, b < n_lon - 1)))
    last = jnp.logical_and(first_lon, jnp.logical_not(is_top))

    pl.when(at_once)(enter)
    loads[0].wait()
    loads[-1].wait()
    outermost = jnp.logical_or(a == 0, is_top)
    pl.when(jnp.logical_and(at_once, outermost))(send_fields)

    load_k.wait()
    load_d.wait()
    kd_src[0, 0:4] = k_v[lon_cells - 4 : lon_cells, :]
    kd_src[0, 4:8] = d_v[lon_cells - 4 : lon_cells, :].astype(F32)
    kd_src[1, 0:4] = k_v[0:4, :]
    kd_src[1, 4:8] = d_v[0:4, :].astype(F32)


    level = sub % 4
    wide_level = lax.broadcasted_iota(jnp.int32, (8, lat_cells), 0) % 4

    for side in range(2):
        tile = slice(lat_cells - LANES, lat_cells) if side == 0 else slice(0, LANES)
        for end, start in ((0, lon_cells - 4), (1, 0)):
            corner = jnp.zeros((8, LANES), F32)
            for r in range(4):
                i = start + r
                k = jnp.broadcast_to(k_v[i : i + 1, tile], (8, LANES))
                d = jnp.broadcast_to(d_v[i : i + 1, tile], (8, LANES))
                weight = jnp.where(d > level, k, 0.0)
                field = jnp.concatenate([x_v[0, i, :, tile], x_v[1, i, :, tile]], axis=0) * weight
                for at, value in ((4 * r, field), (4 * (r + 4), weight)):
                    moved = roll(value, at + (4 if side == 0 else 0))
                    corner = jnp.where(jnp.logical_and(lane >= at, lane < at + 4), moved, corner)
            p_src[side, 2 * parts + end] = corner

    @pl.when(at_once)
    def _():
        send_down()
        pl.when(jnp.logical_not(outermost))(send_fields)
        send_weights()


    def own_weights(i, carry):
        k = jnp.broadcast_to(k_v[pl.ds(i, 1), :], (8, lat_cells))
        d = jnp.broadcast_to(d_v[pl.ds(i, 1), :], (8, lat_cells))
        kw[i + PASSES] = jnp.where(d > wide_level, k, 0.0)
        return carry

    lax.fori_loop(0, lon_cells, own_weights, 0, unroll=17)
    for copy in loads[1:-1]:
        copy.wait()

    def own_fields(i, carry):
        x = jnp.concatenate([x_v[0, i], x_v[1, i]], axis=0)
        y0[i + PASSES] = x * kw[i + PASSES]
        return carry

    lax.fori_loop(0, lon_cells, own_fields, 0, unroll=17)

    def outer(ref, side, row):
        g = row // stride
        if side == 0:
            return roll(ref[row, :, lat_cells - LANES : lat_cells], SLOT * g + 8)
        return roll(ref[row, :, 0:LANES], SLOT * g + 4)

    inside = [spot < 8, jnp.logical_and(spot >= 4, spot < 12)]
    places = ((y0, edge_y), (kw, edge_kw))
    for side in range(2):
        for which, (ref, edge) in enumerate(places):
            pieces = []
            for m in range(stride):
                piece = jnp.zeros((8, LANES), F32)
                for g in range(GROUPS):
                    row = m + stride * g
                    if PASSES <= row < rows - PASSES:
                        piece = jnp.where(lane >= SLOT * g, outer(ref, side, row), piece)
                    elif row >= rows - PASSES:
                        piece = jnp.where(lane >= SLOT * g, 0.0, piece)
                piece = jnp.where(inside[side], piece, 0.0)
                edge[side, m] = piece
                pieces.append(piece)
            for n in range(parts):
                packed = jnp.zeros((8, LANES), F32)
                for t in range(4):
                    if 4 * n + t < stride:
                        packed = jnp.where(spot // 4 == t, roll(pieces[4 * n + t], 4 * t - 4), packed)
                p_src[side, parts * which + n] = packed

    pl.when(jnp.logical_and(at_once, jnp.logical_not(is_top)))(send_edges)

    @pl.when(is_top)
    def _():
        make_strip(stride, p_src, q_src)
        @pl.when(jnp.logical_not(at_once))
        def _():
            enter()

        for copy in strip_straight:
            copy.start()
        for away, copy, slot in strip_mirrored:
            @pl.when(away)
            def _():
                copy.start()

            @pl.when(jnp.logical_not(away))
            def _():
                q_land[slot] = q_src[...]
        send_edges()

        @pl.when(jnp.logical_not(at_once))
        def _():
            send_down()
            send_fields()
            send_weights()

    for copy in small:
        copy.wait()

    @pl.when(is_top)
    def _():
        fold_index(n_lon, lon_cells, b, fp_s, fp_v)

    @pl.when(jnp.logical_and(last, a >= n_lat // 2))
    def _():
        enter()

        @pl.when(has_s)
        def _():
            down[0].start()

        send_down()
        send_fields()
        send_weights()
        send_up()

    for n, ref in enumerate((sigma_s, expand_s)):
        column = jnp.zeros((8, LANES), F32)
        for c in range(2):
            for level in range(4):
                column = jnp.where(sub == 4 * c + level, ref[c, level], column)
        column_out[n] = column
    inverse_out[...] = 1.0 / k_v[...]

    def lattice(ref, row):
        here = [ref[row, :, LANES * t : LANES * (t + 1)] for t in range(tiles)]
        up_one = [roll(v, -1) for v in here]
        down_one = [roll(v, 1) for v in here]
        sums = []
        for t in range(tiles):
            n = jnp.where(lane == LANES - 1, up_one[(t + 1) % tiles], up_one[t])
            s = jnp.where(lane == 0, down_one[t - 1], down_one[t])
            at = slice(LANES * t, LANES * (t + 1))
            sums.append((n + s) + (ref[row + 1, :, at] + ref[row - 1, :, at]))
        return here, sums

    def coefficients(row):
        here, sums = lattice(kw, row)
        for t in range(tiles):
            cc[row, :, LANES * t : LANES * (t + 1)] = 1.0 - here[t] * sums[t]
            qq[row, :, LANES * t : LANES * (t + 1)] = here[t] * here[t]

    states = [y0, y1, y2, y3]

    def advance(step, row):
        here, sums = lattice(states[step], row)
        for t in range(tiles):
            at = slice(LANES * t, LANES * (t + 1))
            new = cc[row, :, at] * here[t] + qq[row, :, at] * sums[t]
            if step < PASSES - 1:
                states[step + 1][row, :, at] = new
            else:
                y_out[row - PASSES, :, at] = new

    def over_rows(first, last, body, unroll):
        def one(row, carry):
            body(row)
            return carry

        lax.fori_loop(first, last, one, 0, unroll=unroll)

    over_rows(PASSES + 1, rows - PASSES - 1, coefficients, 33)
    for step in range(PASSES):
        over_rows(PASSES + 1 + step, rows - PASSES - 1 - step, functools.partial(advance, step), 33 - step)

    @pl.when(jnp.logical_and(last, a < n_lat // 2))
    def _():
        enter()

        @pl.when(has_s)
        def _():
            down[0].start()

        send_down()
        send_fields()
        send_weights()
        send_up()

    @pl.when(has_s)
    def _():
        for copy in up:
            copy.wait_recv()

    @pl.when(jnp.logical_not(has_s))
    def _():
        p_land[0] = jnp.zeros(p_land.shape[1:], F32)
        for n in range(2):
            c_land[n] = jnp.zeros((8, LANES), F32)

    @pl.when(has_n)
    def _():
        for copy in down:
            copy.wait_recv()

    @pl.when(is_top)
    def _():
        p_land[1] = jnp.zeros(p_land.shape[1:], F32)
        for n in range(2, 4):
            c_land[n] = jnp.zeros((8, LANES), F32)

    @pl.when(is_top)
    def _():
        for copy in strip_straight:
            copy.wait_recv()
        for away, copy, _ in strip_mirrored:
            @pl.when(away)
            def _():
                copy.wait_recv()
        fold_strip(n_lon, lon_cells, stride, b, q_src, q_land, fp_v, fold_v)

    for copy in along:
        copy.wait_recv()

    for side, row in ((0, 0), (1, rows - PASSES)):
        for g in range(4):
            k = jnp.broadcast_to(kd_land[side, g : g + 1, :], (8, lat_cells))
            d = jnp.broadcast_to(kd_land[side, 4 + g : 5 + g, :], (8, lat_cells))
            w = jnp.where(d > wide_level.astype(F32), k, 0.0)
            kw[row + g] = w
            x = jnp.concatenate([x_land[side, 0, g], x_land[side, 1, g]], axis=0)
            y0[row + g] = x * w

    beyond = [spot < 4, jnp.logical_and(spot >= 8, spot < 12)]

    def edge_pieces(which, side):
        ref, edge = places[which]
        pieces = []
        for m in range(stride):
            packed = p_land[side, parts * which + m // 4]
            moved = roll(packed, (0 if side == 0 else 8) - 4 * (m % 4))
            pieces.append(jnp.where(beyond[side], moved, edge[1 - side, m]))
        for end, start in ((0, 0), (1, rows - PASSES)):
            corner = c_land[2 * side + end]
            for r in range(4):
                m, g = (start + r) % stride, (start + r) // stride
                at = 4 * (r + 4 * which)
                ghost = roll(corner, (0 if side == 0 else 8) + SLOT * g - at)
                own = jnp.where(inside[1 - side], outer(ref, 1 - side, start + r), 0.0)
                both = jnp.where(beyond[side], ghost, own)
                pieces[m] = jnp.where(lane // SLOT == g, both, pieces[m])
        return pieces

    def edge_sums(pieces):
        sums = []
        for m in range(stride):
            e = pieces[m + 1] if m < stride - 1 else roll(pieces[0], -SLOT)
            w = pieces[m - 1] if m else roll(pieces[stride - 1], SLOT)
            sums.append((roll(pieces[m], -1) + roll(pieces[m], 1)) + (e + w))
        return sums

    def finish(fold):
        def over_fold(step, pieces, side):
            if side == 0 or not fold:
                return pieces
            return [jnp.where(spot == 8, fold_v[step, m], pieces[m]) for m in range(stride)]

        edges, edge_c, edge_q = [], [], []
        for side in range(2):
            weights = over_fold(PASSES, edge_pieces(1, side), side)
            edge_c.append([1.0 - w * total for w, total in zip(weights, edge_sums(weights))])
            edge_q.append([w * w for w in weights])
            edges.append(edge_pieces(0, side))
        for n in range(PASSES):
            coefficients(1 + n)
            coefficients(rows - 2 - n)
        for step in range(PASSES):
            for side in range(2):
                pieces = over_fold(step, edges[side], side)
                edges[side] = [
                    c * y + q * total
                    for c, y, q, total in zip(edge_c[side], pieces, edge_q[side], edge_sums(pieces))
                ]
            for n in range(PASSES):
                advance(step, 1 + step + n)
                advance(step, rows - 2 - step - n)
        for side in range(2):
            for m in range(stride):
                edge_out[side, m] = edges[side][m]

    pl.when(has_n)(functools.partial(finish, False))
    pl.when(is_top)(functools.partial(finish, True))

    for copy in along:
        copy.wait_send()

    @pl.when(has_n)
    def _():
        for copy in up:
            copy.wait_send()

    @pl.when(has_s)
    def _():
        for copy in down:
            copy.wait_send()

    @pl.when(is_top)
    def _():
        for copy in strip_straight:
            copy.wait_send()
        for away, copy, _ in strip_mirrored:
            @pl.when(away)
            def _():
                copy.wait_send()


def balance_kernel(
    y_ref, edge_ref, inverse_ref, column_ref, elev_ref, ratio_ref,
    state_hbm, height_hbm, state_v, whole_v, height_v, sem,
):
    lon_cells, _, lat_cells = y_ref.shape
    stride = edge_ref.shape[1]
    tiles = lat_cells // LANES
    lane, sub = iotas()
    sigma = column_ref[0]
    expand = [jnp.broadcast_to(column_ref[1, s : s + 1, :], (8, LANES)) for s in range(8)]
    copies = []

    def send(src, dst):
        copies.append(pltpu.make_async_copy(src, dst, sem.at[len(copies)]))
        copies[-1].start()

    def balance(i):
        m, g = (i + PASSES) % stride, (i + PASSES) // stride
        for t in range(tiles):
            at = slice(LANES * t, LANES * (t + 1))
            y = y_ref[i, :, at]
            if t == 0:
                y = jnp.where(lane < 4, roll(edge_ref[0, m], -SLOT * g - 4), y)
            if t == tiles - 1:
                y = jnp.where(lane >= LANES - 4, roll(edge_ref[1, m], LANES - 8 - SLOT * g), y)
            scaled = y * (sigma * jnp.broadcast_to(inverse_ref[i : i + 1, at], (8, LANES)))
            ratio = jnp.broadcast_to(ratio_ref[i : i + 1, at], (8, LANES))
            state = scaled + jnp.where(sub >= 4, ratio * pltpu.roll(scaled, 4, 0), 0.0)
            state_v[0, i, :, at] = state[0:4]
            state_v[1, i, :, at] = state[4:8]
            whole_v[t, 8 * i : 8 * i + 8, :] = state

    done = 0
    for start in range(0, lon_cells, 8):
        count = min(8, lon_cells - start)
        for i in range(start, start + count):
            balance(i)
        for t in range(tiles):
            at = slice(LANES * t, LANES * (t + 1))
            height = elev_ref[start : start + count, at]
            for s in range(8):
                height = height + expand[s][0:count] * whole_v[t, pl.ds(8 * start + s, count, stride=8), :]
            height_v[start : start + count, at] = height
        if start + count - done >= 24 or start + count == lon_cells:
            part = pl.ds(done, start + count - done)
            send(state_v.at[:, part], state_hbm.at[:, part])
            done = start + count
    send(height_v, height_hbm)
    for copy in copies:
        copy.wait()


def local(
    n_lon, n_lat,
    control_fields,
    unexplained_elevation,
    diffusivity,
    depth_levels,
    fold_partner,
    prior_sigmas,
    haline_thermal_ratio,
    expansion_coefficients,
):
    levels, lon_cells, lat_cells = control_fields.shape[1:]
    fields = jnp.transpose(control_fields, (0, 2, 1, 3))
    stacked = 2 * levels
    rows = lon_cells + 2 * PASSES
    stride = -(-rows // GROUPS)
    parts = -(-stride // 4)
    vmem = pl.BlockSpec(memory_space=pltpu.VMEM)
    hbm = pl.BlockSpec(memory_space=pltpu.HBM)

    def shape(*dims):
        return jax.ShapeDtypeStruct(dims, F32)

    def tile(*dims):
        return pltpu.VMEM((*dims, 8, LANES), F32)

    def in_hbm(*arrays):
        return [pltpu.with_memory_space_constraint(array, pltpu.HBM) for array in arrays]

    passed = pl.pallas_call(
        functools.partial(diffuse_kernel, n_lon, n_lat),
        name="diffuse",
        out_shape=(
            shape(lon_cells, stacked, lat_cells),
            shape(2, stride, 8, LANES),
            shape(lon_cells, lat_cells),
            shape(2, 8, LANES),
        ),
        in_specs=[hbm] * 6,
        out_specs=(vmem,) * 4,
        scratch_shapes=[
            pltpu.VMEM(fields.shape, F32),
            pltpu.VMEM((lon_cells, lat_cells), F32),
            pltpu.VMEM((lon_cells, lat_cells), jnp.int32),
            pltpu.SMEM(fold_partner.shape, jnp.int32),
            pltpu.SMEM(prior_sigmas.shape, F32),
            pltpu.SMEM(expansion_coefficients.shape, F32),
            pltpu.VMEM((10, 8, LANES), jnp.int32),
            *[pltpu.VMEM((rows, 8, lat_cells), F32) for _ in range(7)],
            tile(2, stride),
            tile(2, stride),
            tile(PASSES + 1, stride),
            pltpu.VMEM((2, 8, lat_cells), F32),
            pltpu.VMEM((2, 2, 4, levels, lat_cells), F32),
            pltpu.VMEM((2, 8, lat_cells), F32),
            tile(2, 2 * parts + 2),
            tile(2, 2 * parts),
            tile(4),
            tile(6),
            tile(10, 6),
            pltpu.SemaphoreType.DMA((9,)),
            pltpu.SemaphoreType.DMA((20,)),
            pltpu.SemaphoreType.DMA((20,)),
            pltpu.SemaphoreType.REGULAR,
        ],
        compiler_params=pltpu.CompilerParams(
            collective_id=0, has_side_effects=True, vmem_limit_bytes=40 * 1024 * 1024
        ),
    )(*in_hbm(fields, diffusivity, depth_levels, fold_partner, prior_sigmas, expansion_coefficients))
    state, height = pl.pallas_call(
        balance_kernel,
        name="balance",
        out_shape=(shape(*fields.shape), shape(lon_cells, lat_cells)),
        in_specs=[vmem] * 6,
        out_specs=(hbm, hbm),
        scratch_shapes=[
            pltpu.VMEM(fields.shape, F32),
            pltpu.VMEM((lat_cells // LANES, 8 * lon_cells, LANES), F32),
            pltpu.VMEM((lon_cells, lat_cells), F32),
            pltpu.SemaphoreType.DMA((8,)),
        ],
        compiler_params=pltpu.CompilerParams(vmem_limit_bytes=40 * 1024 * 1024),
    )(*passed, unexplained_elevation, haline_thermal_ratio)
    return jnp.transpose(state, (0, 2, 1, 3)), height


def solution(mesh):
    return jax.shard_map(
        functools.partial(local, mesh.shape["lon"], mesh.shape["lat"]),
        mesh=mesh,
        in_specs=(
            P(None, None, "lon", "lat"),
            P("lon", "lat"),
            P("lon", "lat"),
            P("lon", "lat"),
            P(),
            P(),
            P("lon", "lat"),
            P(),
        ),
        out_specs=(P(None, None, "lon", "lat"), P("lon", "lat")),
        check_vma=False,
    )
```
